32 devices in a mesh: row: 8 (over y, x, core), col: 4 (over z).
Axes of the slice: x: 2, y: 2, z: 4, core: 2. Of those that a mesh axis runs over, the one named last changes fastest.
Arguments:
- matrix: float32 [16, 1024, 32, 512], P(None, 'row', None, 'col'), may hold values from -21 to 21
Outputs:
- reduced: float32 [16, 1024, 32, 512], P(None, 'row', None, 'col')
- reflectors: float32 [16, 1024, 256], P(None, 'row')
The draws below stay inside these ranges and needn't reach their ends.
All inputs are finite; a program needn't handle non-finite values.
Results may differ from the reference program's by a relative error of at most 0.00011.
Values sent between devices are 32-bit elements; how exact they have to be, the bound alone decides.
A program may use at most 320 MiB of HBM per device.

```python
import jax
import jax.numpy as jnp
from jax import lax

N = 16384
NB = 128
PANELS = 2
RC = 16
CC = 32
N_ROW = 8
N_COL = 4


def draw_matrix(key, part):
    base = jnp.clip(jax.random.normal(key, (N, N), jnp.float32), -6.0, 6.0)
    symmetric = 0.5 * (base + base.T)
    return symmetric.reshape(RC, N_ROW * NB, CC, N_COL * NB)


def setup_inputs(seed: int = 0) -> dict:
    keys = jax.random.split(jax.random.key(seed), 2)
    matrix = draw_matrix(jax.random.fold_in(keys[1], 71), 0)
    return dict(matrix=matrix)


def dot_highest(left, right):
    return jnp.dot(left.astype(jnp.float32), right.astype(jnp.float32), precision=lax.Precision.HIGHEST, preferred_element_type=jnp.float32)

def reference(matrix):
    full = matrix.reshape(N, N)
    identity = jnp.eye(NB, dtype=jnp.float32)
    saved_refl = []
    for panel_idx in range(PANELS):
        first_row = (panel_idx + 1) * NB
        panel_cols = full[first_row:, panel_idx * NB:(panel_idx + 1) * NB]
        gram_sum = dot_highest(panel_cols.T, panel_cols)
        chol_lower = jnp.linalg.cholesky(gram_sum)
        orthonormal = jax.scipy.linalg.solve_triangular(chol_lower, panel_cols.T, lower=True).T
        reflector = jnp.zeros((N, NB), jnp.float32).at[first_row:].set(orthonormal)
        reflector = reflector.at[first_row:first_row + NB].add(-identity)
        kernel = identity - orthonormal[:NB]
        factor = jnp.linalg.cholesky(dot_highest(kernel.T, kernel))
        inverse = jax.scipy.linalg.cho_solve((factor, True), kernel.T)
        product = dot_highest(full, reflector)
        inner_sum = dot_highest(reflector.T, product)
        mixed_core = dot_highest(dot_highest(inverse, inner_sum), inverse.T)
        update = dot_highest(product, inverse.T) - 0.5 * dot_highest(reflector, mixed_core)
        full = full - dot_highest(update, reflector.T) - dot_highest(reflector, update.T)
        saved_refl.append(reflector)
    reduced = full.reshape(matrix.shape)
    bases = jnp.concatenate(saved_refl, axis=1).reshape(matrix.shape[0], matrix.shape[1], PANELS * NB)
    return (reduced, bases)
```

```python
import functools

import jax
import jax.numpy as jnp
from jax import lax
from jax.experimental import pallas as pl
from jax.experimental.pallas import tpu as pltpu
from jax.sharding import PartitionSpec as P

PANELS = 2
MESH = pl.DeviceIdType.MESH
VMEM_LIMIT = 60 * 1024 * 1024


def dot_highest(left, right):
    return jnp.dot(left, right, precision=lax.Precision.HIGHEST, preferred_element_type=jnp.float32)


def greet(*axes):
    barrier = pltpu.get_barrier_semaphore()
    total = 0
    for axis in axes:
        me, size = lax.axis_index(axis), lax.axis_size(axis)
        for step in range(1, size):
            pl.semaphore_signal(
                barrier, inc=1, device_id={axis: lax.rem(me + step, size)}, device_id_type=MESH
            )
        total += size - 1
    pl.semaphore_wait(barrier, total)


def remote(src, dst, send_sem, recv_sem, **device):
    return pltpu.make_async_remote_copy(
        src_ref=src,
        dst_ref=dst,
        send_sem=send_sem,
        recv_sem=recv_sem,
        device_id=device,
        device_id_type=MESH,
    )


def remote_params(collective_id):
    return pltpu.CompilerParams(
        collective_id=collective_id, has_side_effects=True, vmem_limit_bytes=VMEM_LIMIT
    )

STREAM_CHUNKS = 8


def ring_place(pair, pairs):
    return pair + (pair // 2) * (1 - 2 * (pair % 2)) if pairs == 4 else pair


def share_strip(root, strip_ref, out_ref, ring_send, pair_send, recv, local_sem):
    size = lax.axis_size("row")
    me = lax.axis_index("row")
    pairs = size // 2
    piece = out_ref.shape[0] // (2 * STREAM_CHUNKS)
    pair, core = me // 2, me % 2
    place = ring_place(pair, pairs)
    distance = (place - ring_place(root // 2, pairs) + pairs) % pairs
    stream = (core + root % 2) % 2
    hop = (distance * (1 - 2 * stream) + stream * pairs) % pairs
    target = 2 * ring_place((place + 1 - 2 * stream + pairs) % pairs, pairs) + core
    sibling = 2 * pair + 1 - core

    def rows_of(which, i):
        return pl.ds(pl.multiple_of((which * STREAM_CHUNKS + i) * piece, piece), piece)

    def to_ring(i, source, which):
        rows = rows_of(which, i)
        return remote(
            source.at[rows], out_ref.at[rows], ring_send.at[i], recv.at[which, i], row=target
        )

    def to_sibling(i, source, which, slot):
        rows = rows_of(which, i)
        return remote(
            source.at[rows], out_ref.at[rows], pair_send.at[slot, i], recv.at[which, i], row=sibling
        )

    @pl.when(me == root)
    def _():
        own = pltpu.make_async_copy(strip_ref, out_ref, local_sem)
        copies = []
        for i in range(STREAM_CHUNKS):
            copies.append(to_ring(i, strip_ref, 0))
            copies.append(to_sibling(i, strip_ref, 1, 1))
        for i in range(STREAM_CHUNKS):
            copies.append(to_sibling(i, strip_ref, 0, 0))
        for copy in copies:
            copy.start()
        own.start()
        for copy in copies:
            copy.wait_send()
        own.wait()

    @pl.when(me != root)
    def _():
        for i in range(STREAM_CHUNKS):
            onward, across = to_ring(i, out_ref, stream), to_sibling(i, out_ref, stream, 0)
            onward.wait_recv()

            @pl.when(hop < pairs - 1)
            def _():
                onward.start()

            @pl.when(distance > 0)
            def _():
                across.start()

        for i in range(STREAM_CHUNKS):
            to_ring(i, out_ref, 1 - stream).wait_recv()
        for i in range(STREAM_CHUNKS):

            @pl.when(hop < pairs - 1)
            def _():
                to_ring(i, out_ref, stream).wait_send()

            @pl.when(distance > 0)
            def _():
                to_sibling(i, out_ref, stream, 0).wait_send()


STRIP_SEMS = [
    pltpu.SemaphoreType.DMA((STREAM_CHUNKS,)),
    pltpu.SemaphoreType.DMA((2, STREAM_CHUNKS)),
    pltpu.SemaphoreType.DMA((2, STREAM_CHUNKS)),
    pltpu.SemaphoreType.DMA,
]


def strip_kernel(root, layer, a_ref, out_ref, *sems):
    greet("row")
    share_strip(root, a_ref.at[layer], out_ref, *sems)


def spread_strip(matrix, root, layer, collective_id):
    return pl.pallas_call(
        functools.partial(strip_kernel, root, layer),
        out_shape=jax.ShapeDtypeStruct(matrix.shape[1:], matrix.dtype),
        in_specs=[pl.BlockSpec(memory_space=pl.ANY)],
        out_specs=pl.BlockSpec(memory_space=pltpu.VMEM),
        scratch_shapes=STRIP_SEMS,
        compiler_params=remote_params(collective_id),
    )(matrix)


def total_kernel(x_ref, out_ref, held, col_send, col_recv, row_send, row_recv, local_sem):
    rows, cols = lax.axis_size("row"), lax.axis_size("col")
    row, col = lax.axis_index("row"), lax.axis_index("col")
    greet("row", "col")
    own = pltpu.make_async_copy(x_ref.at[row], held.at[col], local_sem)
    own.start()
    copies = []
    for step in range(1, cols):
        copy = remote(
            x_ref.at[row],
            held.at[col],
            col_send.at[step],
            col_recv.at[step],
            col=lax.rem(col + step, cols),
        )
        copy.start()
        copies.append(copy)
    own.wait()
    for copy in copies:
        copy.wait()
    value = held[0]
    for q in range(1, cols):
        value = value + held[q]
    out_ref[row] = value
    copies = []
    for step in range(1, rows):
        copy = remote(
            out_ref.at[row],
            out_ref.at[row],
            row_send.at[step],
            row_recv.at[step],
            row=lax.rem(row + step, rows),
        )
        copy.start()
        copies.append(copy)
    for copy in copies:
        copy.wait()


def total(x, collective_id):
    rows, cols = lax.axis_size("row"), lax.axis_size("col")
    piece = x.shape[0] // rows
    shape = (rows, piece, x.shape[1])
    out = pl.pallas_call(
        total_kernel,
        out_shape=jax.ShapeDtypeStruct(shape, x.dtype),
        in_specs=[pl.BlockSpec(memory_space=pltpu.VMEM)],
        out_specs=pl.BlockSpec(memory_space=pltpu.VMEM),
        scratch_shapes=[
            pltpu.VMEM((cols, piece, x.shape[1]), x.dtype),
            pltpu.SemaphoreType.DMA((cols,)),
            pltpu.SemaphoreType.DMA((cols,)),
            pltpu.SemaphoreType.DMA((rows,)),
            pltpu.SemaphoreType.DMA((rows,)),
            pltpu.SemaphoreType.DMA,
        ],
        compiler_params=remote_params(collective_id),
    )(x.reshape(shape))
    return out.reshape(x.shape)


def product_share_kernel(mirrors, strip, *refs):
    if strip is None:
        part_ref, rows_ref, cols_ref = refs[:3]
        refs = refs[3:]
    else:
        part_ref, a_ref, rows_ref, cols_ref, strip_out = refs[:5]
        refs = refs[5:]
    held, sum_send, sum_recv, all_send, all_recv, tree_send, tree_recv, local_sem = refs[:8]
    rows, cols = lax.axis_size("row"), lax.axis_size("col")
    row, col = lax.axis_index("row"), lax.axis_index("col")
    depth = held.shape[1]
    width = cols_ref.shape[2]
    greet("row", "col")
    copies = []
    for step in range(1, cols):
        peer = lax.rem(col + step, cols)
        copy = remote(
            part_ref.at[peer], held.at[step], sum_send.at[step], sum_recv.at[step], col=peer
        )
        copy.start()
        copies.append(copy)
    if strip is not None:
        root, layer = strip
        share_strip(root, a_ref.at[layer], strip_out, *refs[8:])
    for copy in copies:
        copy.wait()
    value = part_ref[col]
    for step in range(1, cols):
        value = value + held[step]
    rows_ref[col] = value
    copies = []
    for step in range(1, cols):
        copy = remote(
            rows_ref.at[col],
            rows_ref.at[col],
            all_send.at[step],
            all_recv.at[step],
            col=lax.rem(col + step, cols),
        )
        copy.start()
        copies.append(copy)

    bits = rows.bit_length() - 1
    order = [b for b in range(1, bits)] + [0]
    across = [row + (1 - 2 * ((row // 2**b) % 2)) * 2**b for b in order]

    def chunk(mirror, q):
        if depth >= width:
            blocks = depth // width
            return cols_ref.at[pl.ds(q * blocks, blocks), mirror]
        pieces = width // depth
        inside = pl.ds(pl.multiple_of((q % pieces) * depth, depth), depth)
        return cols_ref.at[q // pieces, mirror, inside]

    def source(q):
        view = rows_ref.at[q]
        return view.reshape(depth // width, width, width) if depth >= width else view

    way = 1 - 2 * ((2 * col) // cols)
    visits = []
    for turn in range(cols):
        q = (col + turn * way + cols) % cols
        if turn:
            back = (col - q + cols) % cols
            remote(
                rows_ref.at[q], rows_ref.at[q], all_send.at[0], all_recv.at[back], col=q
            ).wait_recv()
        for mirror in range(mirrors):
            root = col + mirror * cols
            differ = [((row // 2**b) % 2 + (root // 2**b) % 2) % 2 for b in order]
            below = [sum(differ[t:]) for t in range(bits)]
            visits.append((turn, q, mirror, below))

            @pl.when(below[0] == 0)
            def _():
                pltpu.make_async_copy(
                    source(q), chunk(mirror, q), local_sem.at[mirror, turn]
                ).start()
                for t in range(bits):
                    remote(
                        source(q),
                        chunk(mirror, q),
                        tree_send.at[mirror, turn, t],
                        tree_recv.at[mirror, turn],
                        row=across[t],
                    ).start()

            @pl.when(below[0] != 0)
            def _():
                for t in range(bits):
                    copy = remote(
                        chunk(mirror, q),
                        chunk(mirror, q),
                        tree_send.at[mirror, turn, t],
                        tree_recv.at[mirror, turn],
                        row=across[t],
                    )
                    if t == 0:
                        copy.wait_recv()

                    @pl.when(below[t] == 0)
                    def _():
                        copy.start()

    for turn, q, mirror, below in visits:

        @pl.when(below[0] == 0)
        def _():
            pltpu.make_async_copy(source(q), chunk(mirror, q), local_sem.at[mirror, turn]).wait()

        for t in range(bits):

            @pl.when(below[t] == 0)
            def _():
                remote(
                    chunk(mirror, q),
                    chunk(mirror, q),
                    tree_send.at[mirror, turn, t],
                    tree_recv.at[mirror, turn],
                    row=across[t],
                ).wait_send()

    for copy in copies:
        copy.wait_send()


def product_share(part, cyc_rows, strip, matrix, collective_id):
    rows, cols = lax.axis_size("row"), lax.axis_size("col")
    mirrors = rows // cols
    bits = rows.bit_length() - 1
    n_rows, width = part.shape
    depth = n_rows // cols
    out_shape = [
        jax.ShapeDtypeStruct((cols, depth, width), part.dtype),
        jax.ShapeDtypeStruct((cyc_rows, mirrors, width, width), part.dtype),
    ]
    args, specs = [part.reshape(cols, depth, width)], [pl.BlockSpec(memory_space=pltpu.VMEM)]
    scratch = [
        pltpu.VMEM((cols, depth, width), part.dtype),
        pltpu.SemaphoreType.DMA((cols,)),
        pltpu.SemaphoreType.DMA((cols,)),
        pltpu.SemaphoreType.DMA((cols,)),
        pltpu.SemaphoreType.DMA((cols,)),
        pltpu.SemaphoreType.DMA((mirrors, cols, bits)),
        pltpu.SemaphoreType.DMA((mirrors, cols)),
        pltpu.SemaphoreType.DMA((mirrors, cols)),
    ]
    if strip is not None:
        args.append(matrix)
        specs.append(pl.BlockSpec(memory_space=pl.ANY))
        out_shape.append(jax.ShapeDtypeStruct(matrix.shape[1:], matrix.dtype))
        scratch += STRIP_SEMS
    return pl.pallas_call(
        functools.partial(product_share_kernel, mirrors, strip),
        out_shape=out_shape,
        in_specs=specs,
        out_specs=[pl.BlockSpec(memory_space=pltpu.VMEM)] * len(out_shape),
        scratch_shapes=scratch,
        compiler_params=remote_params(collective_id),
    )(*args)


LEAF = 16


def eliminate(ref, symmetric):
    size = ref.shape[0]
    strip_row = lax.broadcasted_iota(jnp.int32, (LEAF, size), 0)
    strip_lane = lax.broadcasted_iota(jnp.int32, (LEAF, size), 1)
    row = lax.broadcasted_iota(jnp.int32, (size, size), 0)
    lane = lax.broadcasted_iota(jnp.int32, (size, size), 1)

    def block(b, carry):
        start = pl.multiple_of(b * LEAF, LEAF)
        whole = ref[...]
        strip = ref[pl.ds(start, LEAF), :]
        columns = [jnp.broadcast_to(strip[:, i : i + 1], (LEAF, size)) for i in range(LEAF)]
        panel = jnp.where(strip_lane < LEAF, (strip_row == strip_lane).astype(jnp.float32), strip)
        for i in range(LEAF):
            column = columns[i]
            pivot = jnp.broadcast_to(column[i : i + 1, :], (LEAF, size))
            if symmetric:
                scale = lax.rsqrt(pivot)
                scale = scale * (1.5 - 0.5 * pivot * scale * scale)
                column = column * scale
                touched = strip_row > i
            else:
                scale = 1.0 / pivot
                touched = strip_row != i

            def step(x):
                lead = jnp.broadcast_to(x[i : i + 1, :], (LEAF, size)) * scale
                return jnp.where(touched, x - column * lead, jnp.where(strip_row == i, lead, x))

            panel = step(panel)
            for j in range(i + 1, LEAF):
                columns[j] = step(columns[j])
        base = jnp.where(lane < LEAF, 0.0, whole)
        if symmetric:
            factor = jnp.where((strip_lane >= LEAF) & (strip_lane < size - start), panel, 0.0)
            factor = pltpu.roll(factor, start, axis=1)
            change = lax.dot_general(
                factor,
                panel,
                (((0,), (0,)), ((), ())),
                precision=lax.Precision.HIGHEST,
                preferred_element_type=jnp.float32,
            )
            ref[...] = jnp.where(row < start, whole, base - change)
        else:
            inside = (row >= start) & (row < start + LEAF)
            factor = jnp.where(inside | (lane >= LEAF), 0.0, whole)
            padded = jnp.concatenate([panel, jnp.zeros((size - LEAF, size), jnp.float32)], axis=0)
            ref[...] = base - dot_highest(factor, padded)
        ref[pl.ds(start, LEAF), :] = panel
        ref[...] = pltpu.roll(ref[...], size - LEAF, axis=1)
        return carry

    lax.fori_loop(0, size // LEAF, block, 0)
    if symmetric:
        ref[...] = jnp.where(row >= lane, ref[...], 0.0)


def transposed_dot(left, right):
    return lax.dot_general(
        left,
        right,
        (((1,), (1,)), ((), ())),
        precision=lax.Precision.HIGHEST,
        preferred_element_type=jnp.float32,
    )


def factor_kernel(both_ref, lower_ref, top_ref, inverse_ref):
    width = both_ref.shape[1]
    lower_ref[...] = both_ref[:width]
    eliminate(lower_ref, True)
    row = lax.broadcasted_iota(jnp.int32, (width, width), 0)
    lane = lax.broadcasted_iota(jnp.int32, (width, width), 1)
    w_top = transposed_dot(both_ref[width:], lower_ref[...]) - (row == lane).astype(jnp.float32)
    top_ref[...] = w_top
    inverse_ref[...] = -w_top
    eliminate(inverse_ref, False)


def factorize(both):
    width = both.shape[1]
    return pl.pallas_call(
        factor_kernel,
        out_shape=[jax.ShapeDtypeStruct((width, width), jnp.float32)] * 3,
        compiler_params=pltpu.CompilerParams(vmem_limit_bytes=VMEM_LIMIT),
    )(both)


def split(value):
    high = value.astype(jnp.bfloat16)
    return high, (value - high.astype(jnp.float32)).astype(jnp.bfloat16)


def split_outside(value):
    high = lax.reduce_precision(value, exponent_bits=8, mantissa_bits=7)
    return high.astype(jnp.bfloat16), (value - high).astype(jnp.bfloat16)


def dot_f32(left, right):
    return jnp.dot(left, right, preferred_element_type=jnp.float32)


def tile_copies(a_ref, held, sems, tile, index, slot):
    return [
        pltpu.make_async_copy(
            a_ref.at[pl.ds(index * tile, tile), c, :], held.at[slot, c], sems.at[slot, c]
        )
        for c in range(a_ref.shape[1])
    ]


def fetch_tiles(a_ref, held, sems, tile):
    step, steps = pl.program_id(0), pl.num_programs(0)
    slot = lax.rem(step, 2)

    @pl.when(step == 0)
    def _():
        for copy in tile_copies(a_ref, held, sems, tile, step, slot):
            copy.start()

    @pl.when(step + 1 < steps)
    def _():
        for copy in tile_copies(a_ref, held, sems, tile, step + 1, 1 - slot):
            copy.start()

    return slot, tile_copies(a_ref, held, sems, tile, step, slot)


def product_kernel(first, group, a_ref, cols_ref, lower_ref, part_ref, w_ref, held, weights, sems):
    tile, width = part_ref.shape
    cyc_cols = a_ref.shape[1]
    slot, copies = fetch_tiles(a_ref, held, sems, tile)

    @pl.when(pl.program_id(0) == 0)
    def _():
        row = lax.broadcasted_iota(jnp.int32, (width, width), 0)
        lane = lax.broadcasted_iota(jnp.int32, (width, width), 1)
        identity = (row == lane).astype(jnp.float32)
        for c in range(cyc_cols):
            rows = slice(c * width, (c + 1) * width)
            here = c * lax.axis_size("col") + lax.axis_index("col")
            w = transposed_dot(cols_ref[rows, :], lower_ref[...])
            w = w - jnp.where(here == first, identity, 0.0)
            w_ref[rows, :] = w
            high, low = split(w)
            weights[rows, :width] = high
            weights[rows, width:] = low

    for copy in copies:
        copy.wait()
    total = None
    for chunk in range(cyc_cols // group):
        parts = [split(held[slot, chunk * group + g]) for g in range(group)]
        high = jnp.concatenate([p[0] for p in parts], axis=1)
        low = jnp.concatenate([p[1] for p in parts], axis=1)
        right = weights[chunk * group * width : (chunk + 1) * group * width, :]
        term = dot_f32(jnp.concatenate([high, low], axis=0), right)
        term = term[:tile] + term[tile:]
        term = term[:, width:] + term[:, :width]
        total = term if total is None else total + term
    part_ref[...] = total


def multiply(matrix, cols, lower, first):
    cyc_rows, width, cyc_cols, _ = matrix.shape
    n_rows = cyc_rows * width
    tile = min(256, n_rows)
    whole = pl.BlockSpec(cols.shape, lambda i: (0, 0), pipeline_mode=pl.Buffered(1))
    return pl.pallas_call(
        functools.partial(product_kernel, first, min(8, cyc_cols)),
        grid=(n_rows // tile,),
        out_shape=[
            jax.ShapeDtypeStruct((n_rows, width), jnp.float32),
            jax.ShapeDtypeStruct(cols.shape, jnp.float32),
        ],
        in_specs=[
            pl.BlockSpec(memory_space=pl.ANY),
            whole,
            pl.BlockSpec((width, width), lambda i: (0, 0)),
        ],
        out_specs=[pl.BlockSpec((tile, width), lambda i: (i, 0)), whole],
        scratch_shapes=[
            pltpu.VMEM((2, cyc_cols, tile, width), jnp.float32),
            pltpu.VMEM((cols.shape[0], 2 * width), jnp.bfloat16),
            pltpu.SemaphoreType.DMA((2, cyc_cols)),
        ],
        compiler_params=pltpu.CompilerParams(vmem_limit_bytes=VMEM_LIMIT),
    )(matrix.reshape(n_rows, cyc_cols, width), cols, lower)


def update_kernel(group, a_ref, u_ref, vh_ref, vl_ref, out_ref, held, done, sems, out_sems):
    tile = u_ref.shape[0]
    cyc_cols, width = a_ref.shape[1:]
    step, steps = pl.program_id(0), pl.num_programs(0)
    slot, copies = fetch_tiles(a_ref, held, sems, tile)
    high, low = split(u_ref[...])

    def stores(index, where):
        return [
            pltpu.make_async_copy(
                done.at[where, c],
                out_ref.at[pl.ds(index * tile, tile), c, :],
                out_sems.at[where, c],
            )
            for c in range(cyc_cols)
        ]

    @pl.when(step >= 2)
    def _():
        for copy in stores(step - 2, slot):
            copy.wait()

    for copy in copies:
        copy.wait()
    started = stores(step, slot)
    for chunk in range(cyc_cols // group):
        columns = slice(chunk * group * width, (chunk + 1) * group * width)
        v_high, v_low = vh_ref[:, columns], vl_ref[:, columns]
        delta = dot_f32(high, v_low) + dot_f32(low, v_high) + dot_f32(high, v_high)
        for g in range(group):
            c = chunk * group + g
            done[slot, c] = held[slot, c] - delta[:, g * width : (g + 1) * width]
            started[c].start()

    @pl.when(step == steps - 1)
    def _():
        for copy in stores(step, slot):
            copy.wait()

        @pl.when(steps > 1)
        def _():
            for copy in stores(step - 1, 1 - slot):
                copy.wait()


def apply_update(matrix, left, right):
    cyc_rows, width, cyc_cols, _ = matrix.shape
    n_rows, depth = left.shape
    tile = min(256, n_rows)
    high, low = split_outside(right.T)
    whole = pl.BlockSpec(high.shape, lambda i: (0, 0), pipeline_mode=pl.Buffered(1))
    held = pltpu.VMEM((2, cyc_cols, tile, width), jnp.float32)
    sems = pltpu.SemaphoreType.DMA((2, cyc_cols))
    return pl.pallas_call(
        functools.partial(update_kernel, min(4, cyc_cols)),
        grid=(n_rows // tile,),
        out_shape=jax.ShapeDtypeStruct((n_rows, cyc_cols, width), jnp.float32),
        in_specs=[
            pl.BlockSpec(memory_space=pl.ANY),
            pl.BlockSpec((tile, depth), lambda i: (i, 0)),
            whole,
            whole,
        ],
        out_specs=pl.BlockSpec(memory_space=pl.ANY),
        scratch_shapes=[held, held, sems, sems],
        compiler_params=pltpu.CompilerParams(vmem_limit_bytes=VMEM_LIMIT),
    )(matrix.reshape(n_rows, cyc_cols, width), left, high, low)


def carry_rows(matrix, count):
    own = matrix[:, :, 0, :].reshape(-1, matrix.shape[3])
    col = lax.axis_index("col")
    last = max(count - 1, 3)
    kept = [own, own]
    moving = own
    for step in range(1, last + 1):
        pairs = [(i, i + 1) for i in (step - 1, step) if i + 1 < count]
        if step == last:
            pairs.append((1, 0))
            moving = jnp.where(col == 1, own, moving)
        moving = lax.ppermute(moving, "col", pairs)
        kept[0] = jnp.where(col == step, moving, kept[0])
        kept[1] = jnp.where(col == step + 1, moving, kept[1])
        if step == last:
            kept[1] = jnp.where(col == 0, moving, kept[1])
    return kept


def local(matrix):
    row_count = lax.axis_size("row")
    col_count = lax.axis_size("col")
    row_index = lax.axis_index("row")
    col_index = lax.axis_index("col")
    cyc_rows, width, cyc_cols, _ = matrix.shape
    n_rows, n_cols = cyc_rows * width, cyc_cols * width
    lanes = jnp.arange(width, dtype=jnp.int32)
    glob_rows = (
        (jnp.arange(cyc_rows, dtype=jnp.int32)[:, None] * row_count + row_index) * width + lanes
    ).reshape(-1)
    glob_cols = (
        (jnp.arange(cyc_cols, dtype=jnp.int32)[:, None] * col_count + col_index) * width + lanes
    ).reshape(-1)

    def columns_of(strip):
        return jnp.transpose(strip, (1, 2, 0)).reshape(n_cols, width)

    raw_rows = carry_rows(matrix, col_count)
    strip = spread_strip(matrix, 0, 0, 0)

    w_rows, w_cols, z_rows, z_cols = [], [], [], []
    w_next, z_next = [], []
    for k in range(PANELS):
        first = (k + 1) * width
        cols, rows = columns_of(strip), raw_rows[k]
        if k:
            inner = jnp.concatenate([w_next[0], z_next[0]], axis=1).T
            cols = cols - dot_highest(jnp.concatenate([z_cols[0], w_cols[0]], axis=1), inner)
            rows = rows - dot_highest(jnp.concatenate([z_rows[0], w_rows[0]], axis=1), inner)
        cols = jnp.where((glob_cols >= first)[:, None], cols, 0.0)
        rows = jnp.where((glob_rows >= first)[:, None], rows, 0.0)
        top_at = ((k + 1) // col_count) * width
        holds_top = col_index == (k + 1) % col_count
        top_part = jnp.where(holds_top, cols[top_at : top_at + width], 0.0)
        both = total(jnp.concatenate([dot_highest(cols.T, cols), top_part], axis=0), 1)
        inv_lower, w_top, inverse = factorize(both)
        part, wc = multiply(matrix, cols, inv_lower, k + 1)
        unit_rows = (glob_rows[:, None] - first == lanes[None, :]).astype(jnp.float32)
        wr = dot_highest(rows, inv_lower.T) - unit_rows
        if k:
            small = dot_highest(jnp.concatenate([w_cols[0], z_cols[0]], axis=1).T, wc)
            part = part - dot_highest(jnp.concatenate([z_rows[0], w_rows[0]], axis=1), small)
        if k + 1 < PANELS:
            next_strip = ((k + 1) % row_count, (k + 1) // row_count)
            y_rows, y_cols, strip = product_share(part, cyc_rows, next_strip, matrix, 2)
        else:
            y_rows, y_cols = product_share(part, cyc_rows, None, matrix, 3)
        y_rows = y_rows.reshape(n_rows, width)
        y_cols = y_cols.reshape(n_cols, width)
        next_part = jnp.where(holds_top, y_cols[top_at : top_at + width], 0.0)
        both = total(jnp.concatenate([dot_highest(wc.T, y_cols), next_part], axis=0), 1)
        middle, y_next = both[:width], both[width:]
        core = 0.5 * dot_highest(dot_highest(inverse, middle), inverse.T)
        finish = jnp.concatenate([inverse.T, -core], axis=0)
        w_rows.append(wr)
        w_cols.append(wc)
        w_next.append(w_top)
        z_rows.append(dot_highest(jnp.concatenate([y_rows, wr], axis=1), finish))
        z_cols.append(dot_highest(jnp.concatenate([y_cols, wc], axis=1), finish))
        z_next.append(dot_highest(jnp.concatenate([y_next, w_top], axis=1), finish))

    left = jnp.concatenate([x for k in range(PANELS) for x in (z_rows[k], w_rows[k])], axis=1)
    right = jnp.concatenate([x for k in range(PANELS) for x in (w_cols[k], z_cols[k])], axis=1)
    reduced = apply_update(matrix, left, right).reshape(matrix.shape)
    bases = jnp.concatenate(w_rows, axis=1).reshape(cyc_rows, width, PANELS * width)
    return (reduced, bases)


def solution(mesh):
    return jax.shard_map(
        local,
        mesh=mesh,
        in_specs=(P(None, "row", None, "col"),),
        out_specs=(P(None, "row", None, "col"), P(None, "row", None)),
        check_vma=False,
    )
```

```python
import functools

import jax
import jax.numpy as jnp
from jax import lax
from jax.experimental import pallas as pl
from jax.experimental.pallas import tpu as pltpu
from jax.sharding import PartitionSpec as P

PANELS = 2
MESH = pl.DeviceIdType.MESH
VMEM_LIMIT = 60 * 1024 * 1024


def dot_highest(left, right):
    return jnp.dot(left, right, precision=lax.Precision.HIGHEST, preferred_element_type=jnp.float32)


def greet(*axes):
    barrier = pltpu.get_barrier_semaphore()
    total = 0
    for axis in axes:
        me, size = lax.axis_index(axis), lax.axis_size(axis)
        for step in range(1, size):
            pl.semaphore_signal(
                barrier, inc=1, device_id={axis: lax.rem(me + step, size)}, device_id_type=MESH
            )
        total += size - 1
    pl.semaphore_wait(barrier, total)


def remote(src, dst, send_sem, recv_sem, **device):
    return pltpu.make_async_remote_copy(
        src_ref=src,
        dst_ref=dst,
        send_sem=send_sem,
        recv_sem=recv_sem,
        device_id=device,
        device_id_type=MESH,
    )


def remote_params(collective_id):
    return pltpu.CompilerParams(
        collective_id=collective_id, has_side_effects=True, vmem_limit_bytes=VMEM_LIMIT
    )

STREAM_CHUNKS = 8

LAG = 2


def ring_place(pair, pairs):
    return pair + (pair // 2) * (1 - 2 * (pair % 2)) if pairs == 4 else pair


class Strip:
    def __init__(self, root, strip_ref, out_ref, ring_send, pair_send, recv, local_sem):
        size = lax.axis_size("row")
        me = lax.axis_index("row")
        pairs = size // 2
        pair, core = me // 2, me % 2
        place = ring_place(pair, pairs)
        distance = (place - ring_place(root // 2, pairs) + pairs) % pairs
        stream = (core + root % 2) % 2
        hop = (distance * (1 - 2 * stream) + stream * pairs) % pairs
        self.target = 2 * ring_place((place + 1 - 2 * stream + pairs) % pairs, pairs) + core
        self.sibling = 2 * pair + 1 - core
        self.root, self.me, self.pairs = root, me, pairs
        self.stream, self.hop, self.distance = stream, hop, distance
        self.strip_ref, self.out_ref = strip_ref, out_ref
        self.ring_send, self.pair_send = ring_send, pair_send
        self.recv, self.local_sem = recv, local_sem
        self.piece = out_ref.shape[0] // (2 * STREAM_CHUNKS)

    def rows_of(self, which, i):
        start = (which * STREAM_CHUNKS + i) * self.piece
        return pl.ds(pl.multiple_of(start, self.piece), self.piece)

    def to_ring(self, i, source, which):
        rows = self.rows_of(which, i)
        return remote(
            source.at[rows],
            self.out_ref.at[rows],
            self.ring_send.at[i],
            self.recv.at[which, i],
            row=self.target,
        )

    def to_sibling(self, i, source, which, slot):
        rows = self.rows_of(which, i)
        return remote(
            source.at[rows],
            self.out_ref.at[rows],
            self.pair_send.at[slot, i],
            self.recv.at[which, i],
            row=self.sibling,
        )

    def root_copies(self):
        copies = []
        for i in range(STREAM_CHUNKS):
            copies.append(self.to_ring(i, self.strip_ref, 0))
            copies.append(self.to_sibling(i, self.strip_ref, 1, 1))
        for i in range(STREAM_CHUNKS):
            copies.append(self.to_sibling(i, self.strip_ref, 0, 0))
        return copies

    def begin(self):
        @pl.when(self.me == self.root)
        def _():
            for copy in self.root_copies():
                copy.start()
            pltpu.make_async_copy(self.strip_ref, self.out_ref, self.local_sem).start()

    def serve(self, i):
        onward = self.to_ring(i, self.out_ref, self.stream)
        onward.wait_recv()

        @pl.when(self.hop < self.pairs - 1)
        def _():
            onward.start()

        @pl.when(self.distance > 0)
        def _():
            self.to_sibling(i, self.out_ref, self.stream, 0).start()

    def serve_turn(self, turn):
        first = 2 * (turn - 2 * self.hop)
        for half in range(2):
            i = first + half

            @pl.when((self.me != self.root) & (i >= 0) & (i < STREAM_CHUNKS))
            def _():
                self.serve(i)

    def turns(self):
        return STREAM_CHUNKS // 2 + 2 * (self.pairs - 1)

    def end(self):
        @pl.when(self.me == self.root)
        def _():
            for copy in self.root_copies():
                copy.wait_send()
            pltpu.make_async_copy(self.strip_ref, self.out_ref, self.local_sem).wait()

        @pl.when(self.me != self.root)
        def _():
            for i in range(STREAM_CHUNKS):
                self.to_ring(i, self.out_ref, 1 - self.stream).wait_recv()

                @pl.when(self.hop < self.pairs - 1)
                def _():
                    self.to_ring(i, self.out_ref, self.stream).wait_send()

                @pl.when(self.distance > 0)
                def _():
                    self.to_sibling(i, self.out_ref, self.stream, 0).wait_send()


STRIP_SEMS = [
    pltpu.SemaphoreType.DMA((STREAM_CHUNKS,)),
    pltpu.SemaphoreType.DMA((2, STREAM_CHUNKS)),
    pltpu.SemaphoreType.DMA((2, STREAM_CHUNKS)),
    pltpu.SemaphoreType.DMA,
]


def strip_kernel(root, layer, a_ref, out_ref, *sems):
    greet("row")
    strip = Strip(root, a_ref.at[layer], out_ref, *sems)
    strip.begin()

    @pl.when(strip.me != root)
    def _():
        for i in range(STREAM_CHUNKS):
            strip.serve(i)

    strip.end()


def spread_strip(matrix, root, layer, collective_id):
    return pl.pallas_call(
        functools.partial(strip_kernel, root, layer),
        out_shape=jax.ShapeDtypeStruct(matrix.shape[1:], matrix.dtype),
        in_specs=[pl.BlockSpec(memory_space=pl.ANY)],
        out_specs=pl.BlockSpec(memory_space=pltpu.VMEM),
        scratch_shapes=STRIP_SEMS,
        compiler_params=remote_params(collective_id),
    )(matrix)


def total_kernel(x_ref, out_ref, held, col_send, col_recv, row_send, row_recv, local_sem):
    rows, cols = lax.axis_size("row"), lax.axis_size("col")
    row, col = lax.axis_index("row"), lax.axis_index("col")
    greet("row", "col")
    own = pltpu.make_async_copy(x_ref.at[row], held.at[col], local_sem)
    own.start()
    copies = []
    for step in range(1, cols):
        copy = remote(
            x_ref.at[row],
            held.at[col],
            col_send.at[step],
            col_recv.at[step],
            col=lax.rem(col + step, cols),
        )
        copy.start()
        copies.append(copy)
    own.wait()
    for copy in copies:
        copy.wait()
    value = held[0]
    for q in range(1, cols):
        value = value + held[q]
    out_ref[row] = value
    copies = []
    for step in range(1, rows):
        copy = remote(
            out_ref.at[row],
            out_ref.at[row],
            row_send.at[step],
            row_recv.at[step],
            row=lax.rem(row + step, rows),
        )
        copy.start()
        copies.append(copy)
    for copy in copies:
        copy.wait()


def total(x, collective_id):
    rows, cols = lax.axis_size("row"), lax.axis_size("col")
    piece = x.shape[0] // rows
    shape = (rows, piece, x.shape[1])
    out = pl.pallas_call(
        total_kernel,
        out_shape=jax.ShapeDtypeStruct(shape, x.dtype),
        in_specs=[pl.BlockSpec(memory_space=pltpu.VMEM)],
        out_specs=pl.BlockSpec(memory_space=pltpu.VMEM),
        scratch_shapes=[
            pltpu.VMEM((cols, piece, x.shape[1]), x.dtype),
            pltpu.SemaphoreType.DMA((cols,)),
            pltpu.SemaphoreType.DMA((cols,)),
            pltpu.SemaphoreType.DMA((rows,)),
            pltpu.SemaphoreType.DMA((rows,)),
            pltpu.SemaphoreType.DMA,
        ],
        compiler_params=remote_params(collective_id),
    )(x.reshape(shape))
    return out.reshape(x.shape)


LEAF = 16


def eliminate(ref, symmetric):
    size = ref.shape[0]
    strip_row = lax.broadcasted_iota(jnp.int32, (LEAF, size), 0)
    strip_lane = lax.broadcasted_iota(jnp.int32, (LEAF, size), 1)
    row = lax.broadcasted_iota(jnp.int32, (size, size), 0)
    lane = lax.broadcasted_iota(jnp.int32, (size, size), 1)

    def block(b, carry):
        start = pl.multiple_of(b * LEAF, LEAF)
        whole = ref[...]
        strip = ref[pl.ds(start, LEAF), :]
        columns = [jnp.broadcast_to(strip[:, i : i + 1], (LEAF, size)) for i in range(LEAF)]
        panel = jnp.where(strip_lane < LEAF, (strip_row == strip_lane).astype(jnp.float32), strip)
        for i in range(LEAF):
            column = columns[i]
            pivot = jnp.broadcast_to(column[i : i + 1, :], (LEAF, size))
            if symmetric:
                scale = lax.rsqrt(pivot)
                scale = scale * (1.5 - 0.5 * pivot * scale * scale)
                column = column * scale
                touched = strip_row > i
            else:
                scale = 1.0 / pivot
                touched = strip_row != i

            def step(x):
                lead = jnp.broadcast_to(x[i : i + 1, :], (LEAF, size)) * scale
                return jnp.where(touched, x - column * lead, jnp.where(strip_row == i, lead, x))

            panel = step(panel)
            for j in range(i + 1, LEAF):
                columns[j] = step(columns[j])
        base = jnp.where(lane < LEAF, 0.0, whole)
        if symmetric:
            factor = jnp.where((strip_lane >= LEAF) & (strip_lane < size - start), panel, 0.0)
            factor = pltpu.roll(factor, start, axis=1)
            change = lax.dot_general(
                factor,
                panel,
                (((0,), (0,)), ((), ())),
                precision=lax.Precision.HIGHEST,
                preferred_element_type=jnp.float32,
            )
            ref[...] = jnp.where(row < start, whole, base - change)
        else:
            inside = (row >= start) & (row < start + LEAF)
            factor = jnp.where(inside | (lane >= LEAF), 0.0, whole)
            padded = jnp.concatenate([panel, jnp.zeros((size - LEAF, size), jnp.float32)], axis=0)
            ref[...] = base - dot_highest(factor, padded)
        ref[pl.ds(start, LEAF), :] = panel
        ref[...] = pltpu.roll(ref[...], size - LEAF, axis=1)
        return carry

    lax.fori_loop(0, size // LEAF, block, 0)
    if symmetric:
        ref[...] = jnp.where(row >= lane, ref[...], 0.0)


def transposed_dot(left, right):
    return lax.dot_general(
        left,
        right,
        (((1,), (1,)), ((), ())),
        precision=lax.Precision.HIGHEST,
        preferred_element_type=jnp.float32,
    )


def factor_kernel(both_ref, lower_ref, top_ref):
    width = both_ref.shape[1]
    lower_ref[...] = both_ref[:width]
    eliminate(lower_ref, True)
    row = lax.broadcasted_iota(jnp.int32, (width, width), 0)
    lane = lax.broadcasted_iota(jnp.int32, (width, width), 1)
    identity = (row == lane).astype(jnp.float32)
    top_ref[...] = transposed_dot(both_ref[width:], lower_ref[...]) - identity


def factorize(both):
    width = both.shape[1]
    return pl.pallas_call(
        factor_kernel,
        out_shape=[jax.ShapeDtypeStruct((width, width), jnp.float32)] * 2,
        compiler_params=pltpu.CompilerParams(vmem_limit_bytes=VMEM_LIMIT),
    )(both)


def split(value):
    high = value.astype(jnp.bfloat16)
    return high, (value - high.astype(jnp.float32)).astype(jnp.bfloat16)


def split_outside(value):
    high = lax.reduce_precision(value, exponent_bits=8, mantissa_bits=7)
    return high.astype(jnp.bfloat16), (value - high).astype(jnp.bfloat16)


def dot_f32(left, right):
    return jnp.dot(left, right, preferred_element_type=jnp.float32)


def tile_copies(a_ref, held, sems, tile, index, slot):
    return [
        pltpu.make_async_copy(
            a_ref.at[pl.ds(index * tile, tile), c, :], held.at[slot, c], sems.at[slot, c]
        )
        for c in range(a_ref.shape[1])
    ]


def fetch_tiles(a_ref, held, sems, tile):
    step, steps = pl.program_id(0), pl.num_programs(0)
    slot = lax.rem(step, 2)

    @pl.when(step == 0)
    def _():
        for copy in tile_copies(a_ref, held, sems, tile, step, slot):
            copy.start()

    @pl.when(step + 1 < steps)
    def _():
        for copy in tile_copies(a_ref, held, sems, tile, step + 1, 1 - slot):
            copy.start()

    return slot, tile_copies(a_ref, held, sems, tile, step, slot)


def transposed_left(left, right):
    return lax.dot_general(
        left, right, (((0,), (0,)), ((), ())), preferred_element_type=jnp.float32
    )


def three_term(left, right, dot):
    high, low = left
    width = right.shape[1] // 2
    wide = dot(high, right)
    return wide[:, width:] + dot(low, right[:, :width]) + wide[:, :width]


def panel_kernel(first, group, mirrors, later, root_strip, *refs):
    refs = list(refs)
    take = lambda n: [refs.pop(0) for _ in range(n)]
    a_ref, cols_ref, lower_ref, top_ref = take(4)
    if later:
        old_cols_ref, old_rows_ref = take(2)
    if root_strip is not None:
        (strip_ref,) = take(1)
    w_ref, inverse_ref, rows_ref, spread_ref = take(4)
    if root_strip is not None:
        (strip_out,) = take(1)
    held, weights, part, arrived, sems = take(5)
    sum_send, sum_recv, on_send, on_recv, tree_send, tree_recv, local_sem = take(7)
    if later:
        small_ref, old_weights = take(2)
    rows, cols = lax.axis_size("row"), lax.axis_size("col")
    row, col = lax.axis_index("row"), lax.axis_index("col")
    cyc_cols, width = a_ref.shape[1:]
    pieces, tile = part.shape[1:3]
    tiles = cols * pieces
    greet("row", "col")

    def owner(index):
        return (col + 1 + index // pieces) % cols

    def fetch(index, slot):
        start = (owner(index) * pieces + index % pieces) * tile
        return [
            pltpu.make_async_copy(
                a_ref.at[pl.ds(pl.multiple_of(start, tile), tile), c, :],
                held.at[slot, c],
                sems.at[slot, c],
            )
            for c in range(cyc_cols)
        ]

    for copy in fetch(0, 0):
        copy.start()
    strip = None
    if root_strip is not None:
        root, layer = root_strip
        strip = Strip(root, strip_ref.at[layer], strip_out, *refs)
        strip.begin()

    square_row = lax.broadcasted_iota(jnp.int32, (width, width), 0)
    square_lane = lax.broadcasted_iota(jnp.int32, (width, width), 1)
    identity = (square_row == square_lane).astype(jnp.float32)
    if later:
        small_ref[...] = jnp.zeros_like(small_ref)

    @pl.loop(0, cyc_cols)
    def _(c):
        where = pl.ds(pl.multiple_of(c * width, width), width)
        w = transposed_dot(cols_ref[where, :], lower_ref[...])
        w = w - identity * (c * cols + col == first).astype(jnp.float32)
        w_ref[where, :] = w
        high, low = split(w)
        both = jnp.concatenate([high, low], axis=1)
        weights[where, :] = both
        if later:
            small_ref[...] += three_term(split(old_cols_ref[where, :]), both, transposed_left)

    if later:
        high, low = split(small_ref[...])
        old_weights[:, :width] = high
        old_weights[:, width:] = low

    def to_owner(index):
        q, piece = owner(index), index % pieces
        return remote(
            part.at[q, piece],
            arrived.at[index // pieces, piece],
            sum_send.at[index],
            sum_recv.at[index],
            col=q,
        )

    @pl.loop(0, tiles)
    def _(index):
        slot = lax.rem(index, 2)

        @pl.when(index + 1 < tiles)
        def _():
            for copy in fetch(index + 1, 1 - slot):
                copy.start()

        for copy in fetch(index, slot):
            copy.wait()
        total = None
        for chunk in range(cyc_cols // group):
            parts = [split(held[slot, chunk * group + g]) for g in range(group)]
            left = tuple(jnp.concatenate([p[i] for p in parts], axis=1) for i in range(2))
            right = weights[chunk * group * width : (chunk + 1) * group * width, :]
            term = three_term(left, right, dot_f32)
            total = term if total is None else total + term
        q, piece = owner(index), index % pieces
        if later:
            start = pl.multiple_of((q * pieces + piece) * tile, tile)
            old = split(old_rows_ref[pl.ds(start, tile), :])
            total = total - three_term(old, old_weights[...], dot_f32)
        part[q, piece] = total

        @pl.when(index < tiles - pieces)
        def _():
            to_owner(index).start()

        if strip is not None:
            strip.serve_turn(index)

    if strip is not None:

        @pl.loop(tiles, max(tiles, strip.turns()))
        def _(turn):
            strip.serve_turn(turn)

    inverse_ref[...] = -top_ref[...]
    eliminate(inverse_ref, False)

    bits = rows.bit_length() - 1
    order = list(range(1, bits)) + [0]
    across = [row + (1 - 2 * ((row // 2**b) % 2)) * 2**b for b in order]

    def spot(mirror, q, piece):
        start = (q * pieces + piece) * tile
        if tile >= width:
            blocks = tile // width
            return spread_ref.at[pl.ds((q * pieces + piece) * blocks, blocks), mirror]
        inside = pl.ds(pl.multiple_of(start % width, tile), tile)
        return spread_ref.at[start // width, mirror, inside]

    def source(q, piece):
        view = rows_ref.at[q, piece]
        return view.reshape(tile // width, width, width) if tile >= width else view

    def onward(q, piece, side):
        return remote(
            rows_ref.at[q, piece],
            rows_ref.at[q, piece],
            on_send.at[side, q, piece],
            on_recv.at[q, piece],
            col=(col + 1 - 2 * side + cols) % cols,
        )

    def branch(mirror, q, piece, t, view):
        return remote(
            view,
            spot(mirror, q, piece),
            tree_send.at[mirror, q, piece, t],
            tree_recv.at[mirror, q, piece],
            row=across[t],
        )

    def own_copy(mirror, q, piece):
        return pltpu.make_async_copy(
            source(q, piece), spot(mirror, q, piece), local_sem.at[mirror, q, piece]
        )

    below = []
    for mirror in range(mirrors):
        root = col + mirror * cols
        differ = [((row // 2**b) % 2 + (root // 2**b) % 2) % 2 for b in order]
        below.append([sum(differ[t:]) for t in range(bits)])

    def root_start(q, piece):
        for mirror in range(mirrors):

            @pl.when(below[mirror][0] == 0)
            def _():
                own_copy(mirror, q, piece).start()
                for t in range(bits):
                    branch(mirror, q, piece, t, source(q, piece)).start()

    def relay(mirror, q, piece):
        for t in range(bits):
            copy = branch(mirror, q, piece, t, spot(mirror, q, piece))
            if t == 0:
                copy.wait_recv()

            @pl.when(below[mirror][t] == 0)
            def _():
                copy.start()

    @pl.loop(0, pieces)
    def _(piece):
        value = part[col, piece]
        for step in range(cols - 1):
            to_owner(step * pieces + piece).wait_recv()
            value = value + arrived[step, piece]
        rows_ref[col, piece] = value
        for side in range(2):

            @pl.when((col < cols - 1) if side == 0 else (col > 0))
            def _():
                onward(col, piece, side).start()

    both_sides = jnp.minimum(col, cols - 1 - col)
    longer = jnp.where(2 * col < cols - 1, 1, -1)

    def visit(number):
        group, piece = number // pieces, number % pieces
        paired = group <= 2 * both_sides
        far = jnp.where(paired, (group + 1) // 2, group - both_sides)
        way = jnp.where(paired, 1 - 2 * (group % 2), longer)
        return col + far * way, piece, way

    visits = cols * pieces
    lags = [LAG * below[mirror][0] for mirror in range(mirrors)]

    @pl.loop(0, visits + LAG * bits)
    def _(number):
        q, piece, way = visit(number)

        @pl.when(number < visits)
        def _():
            for side in range(2):

                @pl.when((number >= pieces) & (way == 1 - 2 * (1 - side)))
                def _():
                    copy = onward(q, piece, side)
                    copy.wait_recv()

                    @pl.when((col < cols - 1) if side == 0 else (col > 0))
                    def _():
                        copy.start()

            root_start(q, piece)

        for mirror in range(mirrors):
            late = number - lags[mirror]

            @pl.when((below[mirror][0] != 0) & (late >= 0) & (late < visits))
            def _():
                q, piece, _way = visit(late)
                relay(mirror, q, piece)

    @pl.loop(0, cols)
    def _(q):
        @pl.loop(0, pieces)
        def _(piece):
            @pl.when((q <= col) & (col < cols - 1))
            def _():
                onward(q, piece, 0).wait_send()

            @pl.when((q >= col) & (col > 0))
            def _():
                onward(q, piece, 1).wait_send()

            for mirror in range(mirrors):

                @pl.when(below[mirror][0] == 0)
                def _():
                    own_copy(mirror, q, piece).wait()

                for t in range(bits):

                    @pl.when(below[mirror][t] == 0)
                    def _():
                        branch(mirror, q, piece, t, spot(mirror, q, piece)).wait_send()

    @pl.loop(0, tiles - pieces)
    def _(index):
        to_owner(index).wait_send()

    if strip is not None:
        strip.end()


def panel_product(matrix, cols, lower, w_top, first, old, root_strip, collective_id):
    rows_size, cols_size = lax.axis_size("row"), lax.axis_size("col")
    mirrors = rows_size // cols_size
    bits = rows_size.bit_length() - 1
    cyc_rows, width, cyc_cols, _ = matrix.shape
    n_rows = cyc_rows * width
    depth = n_rows // cols_size
    tile = min(256, depth)
    pieces = depth // tile
    flat = matrix.reshape(n_rows, cyc_cols, width)
    vmem, anywhere = pl.BlockSpec(memory_space=pltpu.VMEM), pl.BlockSpec(memory_space=pl.ANY)
    f32, dma = jnp.float32, pltpu.SemaphoreType.DMA
    args, specs = [flat, cols, lower, w_top], [anywhere, vmem, vmem, vmem]
    if old is not None:
        args += list(old)
        specs += [vmem, vmem]
    out_shape = [
        jax.ShapeDtypeStruct(cols.shape, f32),
        jax.ShapeDtypeStruct((width, width), f32),
        jax.ShapeDtypeStruct((cols_size, pieces, tile, width), f32),
        jax.ShapeDtypeStruct((cyc_rows, mirrors, width, width), f32),
    ]
    scratch = [
        pltpu.VMEM((2, cyc_cols, tile, width), f32),
        pltpu.VMEM((cols.shape[0], 2 * width), jnp.bfloat16),
        pltpu.VMEM((cols_size, pieces, tile, width), f32),
        pltpu.VMEM((cols_size - 1, pieces, tile, width), f32),
        dma((2, cyc_cols)),
        dma((cols_size * pieces,)),
        dma((cols_size * pieces,)),
        dma((2, cols_size, pieces)),
        dma((cols_size, pieces)),
        dma((mirrors, cols_size, pieces, bits)),
        dma((mirrors, cols_size, pieces)),
        dma((mirrors, cols_size, pieces)),
    ]
    if old is not None:
        scratch += [
            pltpu.VMEM((2 * width, width), f32),
            pltpu.VMEM((2 * width, 2 * width), jnp.bfloat16),
        ]
    if root_strip is not None:
        args.append(matrix)
        specs.append(anywhere)
        out_shape.append(jax.ShapeDtypeStruct(matrix.shape[1:], f32))
        scratch += STRIP_SEMS
    return pl.pallas_call(
        functools.partial(
            panel_kernel, first, min(8, cyc_cols), mirrors, old is not None, root_strip
        ),
        out_shape=out_shape,
        in_specs=specs,
        out_specs=[vmem] * len(out_shape),
        scratch_shapes=scratch,
        compiler_params=remote_params(collective_id),
    )(*args)


def update_kernel(group, a_ref, u_ref, vh_ref, vl_ref, out_ref, held, done, sems, out_sems):
    tile = u_ref.shape[0]
    cyc_cols, width = a_ref.shape[1:]
    step, steps = pl.program_id(0), pl.num_programs(0)
    slot, copies = fetch_tiles(a_ref, held, sems, tile)
    high, low = split(u_ref[...])

    def stores(index, where):
        return [
            pltpu.make_async_copy(
                done.at[where, c],
                out_ref.at[pl.ds(index * tile, tile), c, :],
                out_sems.at[where, c],
            )
            for c in range(cyc_cols)
        ]

    @pl.when(step >= 2)
    def _():
        for copy in stores(step - 2, slot):
            copy.wait()

    for copy in copies:
        copy.wait()
    started = stores(step, slot)
    for chunk in range(cyc_cols // group):
        columns = slice(chunk * group * width, (chunk + 1) * group * width)
        v_high, v_low = vh_ref[:, columns], vl_ref[:, columns]
        delta = dot_f32(high, v_low) + dot_f32(low, v_high) + dot_f32(high, v_high)
        for g in range(group):
            c = chunk * group + g
            done[slot, c] = held[slot, c] - delta[:, g * width : (g + 1) * width]
            started[c].start()

    @pl.when(step == steps - 1)
    def _():
        for copy in stores(step, slot):
            copy.wait()

        @pl.when(steps > 1)
        def _():
            for copy in stores(step - 1, 1 - slot):
                copy.wait()


def apply_update(matrix, left, right):
    cyc_rows, width, cyc_cols, _ = matrix.shape
    n_rows, depth = left.shape
    tile = min(256, n_rows)
    high, low = split_outside(right.T)
    whole = pl.BlockSpec(high.shape, lambda i: (0, 0), pipeline_mode=pl.Buffered(1))
    held = pltpu.VMEM((2, cyc_cols, tile, width), jnp.float32)
    sems = pltpu.SemaphoreType.DMA((2, cyc_cols))
    return pl.pallas_call(
        functools.partial(update_kernel, min(4, cyc_cols)),
        grid=(n_rows // tile,),
        out_shape=jax.ShapeDtypeStruct((n_rows, cyc_cols, width), jnp.float32),
        in_specs=[
            pl.BlockSpec(memory_space=pl.ANY),
            pl.BlockSpec((tile, depth), lambda i: (i, 0)),
            whole,
            whole,
        ],
        out_specs=pl.BlockSpec(memory_space=pl.ANY),
        scratch_shapes=[held, held, sems, sems],
        compiler_params=pltpu.CompilerParams(vmem_limit_bytes=VMEM_LIMIT),
    )(matrix.reshape(n_rows, cyc_cols, width), left, high, low)


def carry_rows(matrix, count):
    own = matrix[:, :, 0, :].reshape(-1, matrix.shape[3])
    col = lax.axis_index("col")
    last = max(count - 1, 3)
    kept = [own, own]
    moving = own
    for step in range(1, last + 1):
        pairs = [(i, i + 1) for i in (step - 1, step) if i + 1 < count]
        if step == last:
            pairs.append((1, 0))
            moving = jnp.where(col == 1, own, moving)
        moving = lax.ppermute(moving, "col", pairs)
        kept[0] = jnp.where(col == step, moving, kept[0])
        kept[1] = jnp.where(col == step + 1, moving, kept[1])
        if step == last:
            kept[1] = jnp.where(col == 0, moving, kept[1])
    return kept


def local(matrix):
    row_count = lax.axis_size("row")
    col_count = lax.axis_size("col")
    row_index = lax.axis_index("row")
    col_index = lax.axis_index("col")
    cyc_rows, width, cyc_cols, _ = matrix.shape
    n_rows, n_cols = cyc_rows * width, cyc_cols * width
    lanes = jnp.arange(width, dtype=jnp.int32)
    glob_rows = (
        (jnp.arange(cyc_rows, dtype=jnp.int32)[:, None] * row_count + row_index) * width + lanes
    ).reshape(-1)
    glob_cols = (
        (jnp.arange(cyc_cols, dtype=jnp.int32)[:, None] * col_count + col_index) * width + lanes
    ).reshape(-1)

    def columns_of(strip):
        return jnp.transpose(strip, (1, 2, 0)).reshape(n_cols, width)

    raw_rows = carry_rows(matrix, col_count)
    strip = spread_strip(matrix, 0, 0, 0)

    w_rows, w_cols, z_rows, z_cols = [], [], [], []
    w_next, z_next = [], []
    for k in range(PANELS):
        first = (k + 1) * width
        cols, rows = columns_of(strip), raw_rows[k]
        if k:
            inner = jnp.concatenate([w_next[0], z_next[0]], axis=1).T
            cols = cols - dot_highest(jnp.concatenate([z_cols[0], w_cols[0]], axis=1), inner)
            rows = rows - dot_highest(jnp.concatenate([z_rows[0], w_rows[0]], axis=1), inner)
        cols = jnp.where((glob_cols >= first)[:, None], cols, 0.0)
        rows = jnp.where((glob_rows >= first)[:, None], rows, 0.0)
        top_at = ((k + 1) // col_count) * width
        holds_top = col_index == (k + 1) % col_count
        top_part = jnp.where(holds_top, cols[top_at : top_at + width], 0.0)
        both = total(jnp.concatenate([dot_highest(cols.T, cols), top_part], axis=0), 1)
        inv_lower, w_top = factorize(both)
        unit_rows = (glob_rows[:, None] - first == lanes[None, :]).astype(jnp.float32)
        wr = dot_highest(rows, inv_lower.T) - unit_rows
        old = None
        if k:
            old = (
                jnp.concatenate([w_cols[0], z_cols[0]], axis=1),
                jnp.concatenate([z_rows[0], w_rows[0]], axis=1),
            )
        strip_of = ((k + 1) % row_count, (k + 1) // row_count) if k + 1 < PANELS else None
        wc, inverse, y_rows, y_cols, *rest = panel_product(
            matrix, cols, inv_lower, w_top, k + 1, old, strip_of, 2 + k
        )
        strip = rest[0] if rest else None
        y_rows = y_rows.reshape(n_rows, width)
        y_cols = y_cols.reshape(n_cols, width)
        next_part = jnp.where(holds_top, y_cols[top_at : top_at + width], 0.0)
        both = total(jnp.concatenate([dot_highest(wc.T, y_cols), next_part], axis=0), 1)
        middle, y_next = both[:width], both[width:]
        core = 0.5 * dot_highest(dot_highest(inverse, middle), inverse.T)
        finish = jnp.concatenate([inverse.T, -core], axis=0)
        w_rows.append(wr)
        w_cols.append(wc)
        w_next.append(w_top)
        z_rows.append(dot_highest(jnp.concatenate([y_rows, wr], axis=1), finish))
        z_cols.append(dot_highest(jnp.concatenate([y_cols, wc], axis=1), finish))
        z_next.append(dot_highest(jnp.concatenate([y_next, w_top], axis=1), finish))

    left = jnp.concatenate([x for k in range(PANELS) for x in (z_rows[k], w_rows[k])], axis=1)
    right = jnp.concatenate([x for k in range(PANELS) for x in (w_cols[k], z_cols[k])], axis=1)
    reduced = apply_update(matrix, left, right).reshape(matrix.shape)
    bases = jnp.concatenate(w_rows, axis=1).reshape(cyc_rows, width, PANELS * width)
    return (reduced, bases)


def solution(mesh):
    return jax.shard_map(
        local,
        mesh=mesh,
        in_specs=(P(None, "row", None, "col"),),
        out_specs=(P(None, "row", None, "col"), P(None, "row", None)),
        check_vma=False,
    )
```

```python
import functools

import jax
import jax.numpy as jnp
from jax import lax
from jax.experimental import pallas as pl
from jax.experimental.pallas import tpu as pltpu
from jax.sharding import PartitionSpec as P

PANELS = 2
MESH = pl.DeviceIdType.MESH
VMEM_LIMIT = 60 * 1024 * 1024


def dot_highest(left, right):
    return jnp.dot(left, right, precision=lax.Precision.HIGHEST, preferred_element_type=jnp.float32)


def greet(*axes):
    barrier = pltpu.get_barrier_semaphore()
    total = 0
    for axis in axes:
        me, size = lax.axis_index(axis), lax.axis_size(axis)
        for step in range(1, size):
            pl.semaphore_signal(
                barrier, inc=1, device_id={axis: lax.rem(me + step, size)}, device_id_type=MESH
            )
        total += size - 1
    pl.semaphore_wait(barrier, total)


def remote(src, dst, send_sem, recv_sem, **device):
    return pltpu.make_async_remote_copy(
        src_ref=src,
        dst_ref=dst,
        send_sem=send_sem,
        recv_sem=recv_sem,
        device_id=device,
        device_id_type=MESH,
    )


def remote_params(collective_id):
    return pltpu.CompilerParams(
        collective_id=collective_id, has_side_effects=True, vmem_limit_bytes=VMEM_LIMIT
    )

STREAM_CHUNKS = 8

LAG = 2


def ring_place(pair, pairs):
    return pair + (pair // 2) * (1 - 2 * (pair % 2)) if pairs == 4 else pair


class Strip:
    def __init__(self, root, strip_ref, out_ref, ring_send, pair_send, recv, local_sem):
        size = lax.axis_size("row")
        me = lax.axis_index("row")
        pairs = size // 2
        pair, core = me // 2, me % 2
        place = ring_place(pair, pairs)
        distance = (place - ring_place(root // 2, pairs) + pairs) % pairs
        stream = (core + root % 2) % 2
        hop = (distance * (1 - 2 * stream) + stream * pairs) % pairs
        self.target = 2 * ring_place((place + 1 - 2 * stream + pairs) % pairs, pairs) + core
        self.sibling = 2 * pair + 1 - core
        self.root, self.me, self.pairs = root, me, pairs
        self.stream, self.hop, self.distance = stream, hop, distance
        self.strip_ref, self.out_ref = strip_ref, out_ref
        self.ring_send, self.pair_send = ring_send, pair_send
        self.recv, self.local_sem = recv, local_sem
        self.piece = out_ref.shape[0] // (2 * STREAM_CHUNKS)

    def rows_of(self, which, i):
        start = (which * STREAM_CHUNKS + i) * self.piece
        return pl.ds(pl.multiple_of(start, self.piece), self.piece)

    def to_ring(self, i, source, which):
        rows = self.rows_of(which, i)
        return remote(
            source.at[rows],
            self.out_ref.at[rows],
            self.ring_send.at[i],
            self.recv.at[which, i],
            row=self.target,
        )

    def to_sibling(self, i, source, which, slot):
        rows = self.rows_of(which, i)
        return remote(
            source.at[rows],
            self.out_ref.at[rows],
            self.pair_send.at[slot, i],
            self.recv.at[which, i],
            row=self.sibling,
        )

    def root_copies(self):
        copies = []
        for i in range(STREAM_CHUNKS):
            copies.append(self.to_ring(i, self.strip_ref, 0))
            copies.append(self.to_sibling(i, self.strip_ref, 1, 1))
        for i in range(STREAM_CHUNKS):
            copies.append(self.to_sibling(i, self.strip_ref, 0, 0))
        return copies

    def begin(self):
        @pl.when(self.me == self.root)
        def _():
            for copy in self.root_copies():
                copy.start()
            pltpu.make_async_copy(self.strip_ref, self.out_ref, self.local_sem).start()

    def serve(self, i):
        onward = self.to_ring(i, self.out_ref, self.stream)
        onward.wait_recv()

        @pl.when(self.hop < self.pairs - 1)
        def _():
            onward.start()

        @pl.when(self.distance > 0)
        def _():
            self.to_sibling(i, self.out_ref, self.stream, 0).start()

    def serve_turn(self, turn):
        first = 2 * (turn - 2 * self.hop)
        for half in range(2):
            i = first + half

            @pl.when((self.me != self.root) & (i >= 0) & (i < STREAM_CHUNKS))
            def _():
                self.serve(i)

    def turns(self):
        return STREAM_CHUNKS // 2 + 2 * (self.pairs - 1)

    def end(self):
        @pl.when(self.me == self.root)
        def _():
            for copy in self.root_copies():
                copy.wait_send()
            pltpu.make_async_copy(self.strip_ref, self.out_ref, self.local_sem).wait()

        @pl.when(self.me != self.root)
        def _():
            for i in range(STREAM_CHUNKS):
                self.to_ring(i, self.out_ref, 1 - self.stream).wait_recv()

                @pl.when(self.hop < self.pairs - 1)
                def _():
                    self.to_ring(i, self.out_ref, self.stream).wait_send()

                @pl.when(self.distance > 0)
                def _():
                    self.to_sibling(i, self.out_ref, self.stream, 0).wait_send()


STRIP_SEMS = [
    pltpu.SemaphoreType.DMA((STREAM_CHUNKS,)),
    pltpu.SemaphoreType.DMA((2, STREAM_CHUNKS)),
    pltpu.SemaphoreType.DMA((2, STREAM_CHUNKS)),
    pltpu.SemaphoreType.DMA,
]


class Chain:
    def __init__(self, root, layer, a_ref, out_ref, send, recv, local_sems):
        self.col, self.cols = lax.axis_index("col"), lax.axis_size("col")
        self.root, self.layer, self.a_ref, self.out_ref = root, layer, a_ref, out_ref
        self.send, self.recv, self.local_sems = send, recv, local_sems
        self.count = recv.shape[0]
        self.piece = out_ref.shape[0] // self.count
        self.ways = [(self.col >= root) & (self.col < self.cols - 1), (self.col <= root) & (self.col > 0)]

    def part(self, i):
        return pl.ds(pl.multiple_of(i * self.piece, self.piece), self.piece)

    def local(self, i):
        return pltpu.make_async_copy(
            self.a_ref.at[self.part(i), :, self.layer, :],
            self.out_ref.at[self.part(i)],
            self.local_sems.at[i],
        )

    def onward(self, i, side):
        view = self.out_ref.at[self.part(i)]
        target = (self.col + 1 - 2 * side + self.cols) % self.cols
        return remote(view, view, self.send.at[side, i], self.recv.at[i], col=target)

    def begin(self):
        @pl.when(self.col == self.root)
        def _():
            for i in range(self.count):
                self.local(i).start()
            for i in range(self.count):
                self.local(i).wait()
                for side in range(2):

                    @pl.when(self.ways[side])
                    def _():
                        self.onward(i, side).start()

    def serve(self, i):
        @pl.when(self.col != self.root)
        def _():
            self.onward(i, 0).wait_recv()
            for side in range(2):

                @pl.when(self.ways[side])
                def _():
                    self.onward(i, side).start()

    def serve_turn(self, turn):
        far = jnp.maximum(self.col - self.root, self.root - self.col)
        i = turn - far

        @pl.when((i >= 0) & (i < self.count))
        def _():
            self.serve(i)

    def turns(self):
        return self.count + self.cols

    def end(self):
        for i in range(self.count):
            for side in range(2):

                @pl.when(self.ways[side])
                def _():
                    self.onward(i, side).wait_send()


def chain_sems(cyc_rows):
    count = min(8, cyc_rows)
    dma = pltpu.SemaphoreType.DMA
    return [dma((2, count)), dma((count,)), dma((count,))]


def spread_kernel(root, layer, col_root, col_layer, a_ref, strip_ref, rows_ref, *sems):
    greet("row", "col")
    strip = Strip(root, a_ref.at[layer], strip_ref, *sems[: len(STRIP_SEMS)])
    chain = Chain(col_root, col_layer, a_ref, rows_ref, *sems[len(STRIP_SEMS) :])
    strip.begin()
    chain.begin()

    @pl.loop(0, max(strip.turns(), chain.turns()))
    def _(turn):
        chain.serve_turn(turn)
        strip.serve_turn(turn)

    strip.end()
    chain.end()


def spread(matrix, root, layer, col_root, col_layer, collective_id):
    cyc_rows, width, _, _ = matrix.shape
    return pl.pallas_call(
        functools.partial(spread_kernel, root, layer, col_root, col_layer),
        out_shape=[
            jax.ShapeDtypeStruct(matrix.shape[1:], matrix.dtype),
            jax.ShapeDtypeStruct((cyc_rows, width, width), matrix.dtype),
        ],
        in_specs=[pl.BlockSpec(memory_space=pl.ANY)],
        out_specs=[pl.BlockSpec(memory_space=pltpu.VMEM)] * 2,
        scratch_shapes=STRIP_SEMS + chain_sems(cyc_rows),
        compiler_params=remote_params(collective_id),
    )(matrix)


def sum_over_col(x_ref, out_ref, held, col_send, col_recv, row_send, row_recv, between=None):
    rows, cols = lax.axis_size("row"), lax.axis_size("col")
    row, col = lax.axis_index("row"), lax.axis_index("col")
    copies = []
    for step in range(1, cols):
        copy = remote(
            x_ref.at[row],
            held.at[col],
            col_send.at[step],
            col_recv.at[step],
            col=lax.rem(col + step, cols),
        )
        copy.start()
        copies.append(copy)
    held[col] = x_ref[row]
    for copy in copies:
        copy.wait()
    value = held[0]
    for q in range(1, cols):
        value = value + held[q]
    out_ref[row] = value
    copies = []
    for step in range(1, rows):
        copy = remote(
            out_ref.at[row],
            out_ref.at[row],
            row_send.at[step],
            row_recv.at[step],
            row=lax.rem(row + step, rows),
        )
        copy.start()
        copies.append(copy)
    if between is not None:
        between()
    for copy in copies:
        copy.wait()


def sum_scratch(width):
    rows, cols = lax.axis_size("row"), lax.axis_size("col")
    piece = 2 * width // rows
    dma = pltpu.SemaphoreType.DMA
    return [
        pltpu.VMEM((rows, piece, width), jnp.float32),
        pltpu.VMEM((cols, piece, width), jnp.float32),
        dma((cols,)),
        dma((cols,)),
        dma((rows,)),
        dma((rows,)),
    ]


def put_half(x_ref, half, value):
    rows, piece, width = x_ref.shape
    for r in range(rows // 2):
        x_ref[half * (rows // 2) + r] = value[r * piece : (r + 1) * piece]


def get_half(x_ref, half):
    rows, piece, width = x_ref.shape
    return x_ref[pl.ds(half * (rows // 2), rows // 2)].reshape(width, width)


LEAF = 16


def eliminate(ref, symmetric, beside=None):
    size = ref.shape[0]
    strip_row = lax.broadcasted_iota(jnp.int32, (LEAF, size), 0)
    strip_lane = lax.broadcasted_iota(jnp.int32, (LEAF, size), 1)
    row = lax.broadcasted_iota(jnp.int32, (size, size), 0)
    lane = lax.broadcasted_iota(jnp.int32, (size, size), 1)

    def block(b, carry):
        start = pl.multiple_of(b * LEAF, LEAF)
        whole = ref[...]
        strip = ref[pl.ds(start, LEAF), :]
        columns = [jnp.broadcast_to(strip[:, i : i + 1], (LEAF, size)) for i in range(LEAF)]
        panel = jnp.where(strip_lane < LEAF, (strip_row == strip_lane).astype(jnp.float32), strip)
        for i in range(LEAF):
            column = columns[i]
            pivot = jnp.broadcast_to(column[i : i + 1, :], (LEAF, size))
            if symmetric:
                scale = lax.rsqrt(pivot)
                scale = scale * (1.5 - 0.5 * pivot * scale * scale)
                column = column * scale
                touched = strip_row > i
            else:
                scale = 1.0 / pivot
                touched = strip_row != i

            def step(x):
                lead = jnp.broadcast_to(x[i : i + 1, :], (LEAF, size)) * scale
                return jnp.where(touched, x - column * lead, jnp.where(strip_row == i, lead, x))

            panel = step(panel)
            for j in range(i + 1, LEAF):
                columns[j] = step(columns[j])
        base = jnp.where(lane < LEAF, 0.0, whole)
        if symmetric:
            factor = jnp.where((strip_lane >= LEAF) & (strip_lane < size - start), panel, 0.0)
            factor = pltpu.roll(factor, start, axis=1)
            change = lax.dot_general(
                factor,
                panel,
                (((0,), (0,)), ((), ())),
                precision=lax.Precision.HIGHEST,
                preferred_element_type=jnp.float32,
            )
            ref[...] = jnp.where(row < start, whole, base - change)
        else:
            inside = (row >= start) & (row < start + LEAF)
            factor = jnp.where(inside | (lane >= LEAF), 0.0, whole)
            padded = jnp.concatenate([panel, jnp.zeros((size - LEAF, size), jnp.float32)], axis=0)
            ref[...] = base - dot_highest(factor, padded)
        ref[pl.ds(start, LEAF), :] = panel
        ref[...] = pltpu.roll(ref[...], size - LEAF, axis=1)
        if beside is not None:
            beside(b)
        return carry

    lax.fori_loop(0, size // LEAF, block, 0)
    if symmetric:
        ref[...] = jnp.where(row >= lane, ref[...], 0.0)


def transposed_dot(left, right):
    return lax.dot_general(
        left,
        right,
        (((1,), (1,)), ((), ())),
        precision=lax.Precision.HIGHEST,
        preferred_element_type=jnp.float32,
    )


def split(value):
    high = value.astype(jnp.bfloat16)
    return high, (value - high.astype(jnp.float32)).astype(jnp.bfloat16)


def dot_f32(left, right):
    return jnp.dot(left, right, preferred_element_type=jnp.float32)


def tile_copies(a_ref, held, sems, tile, index, slot):
    return [
        pltpu.make_async_copy(
            a_ref.at[pl.ds(index * tile, tile), c, :], held.at[slot, c], sems.at[slot, c]
        )
        for c in range(a_ref.shape[1])
    ]


def fetch_tiles(a_ref, held, sems, tile):
    step, steps = pl.program_id(0), pl.num_programs(0)
    slot = lax.rem(step, 2)

    @pl.when(step == 0)
    def _():
        for copy in tile_copies(a_ref, held, sems, tile, step, slot):
            copy.start()

    @pl.when(step + 1 < steps)
    def _():
        for copy in tile_copies(a_ref, held, sems, tile, step + 1, 1 - slot):
            copy.start()

    return slot, tile_copies(a_ref, held, sems, tile, step, slot)


def transposed_left(left, right):
    return lax.dot_general(
        left, right, (((0,), (0,)), ((), ())), preferred_element_type=jnp.float32
    )


def three_term(left, right, dot):
    high, low = left
    width = right.shape[1] // 2
    wide = dot(high, right)
    return wide[:, width:] + dot(low, right[:, :width]) + wide[:, :width]


def eye(width):
    row = lax.broadcasted_iota(jnp.int32, (width, width), 0)
    lane = lax.broadcasted_iota(jnp.int32, (width, width), 1)
    return (row == lane).astype(jnp.float32)


def flag(condition):
    return condition.astype(jnp.float32)


def side_by_side(value):
    return jnp.concatenate(split(value), axis=1)


def prepare_kernel(first, later, chain_root, *refs):
    refs = list(refs)
    take = lambda n: [refs.pop(0) for _ in range(n)]
    strip_ref, raw_rows_ref = take(2)
    if later:
        both_ref, inverse_ref, old_top_ref, y_cols_ref, w_cols_ref, y_rows_ref, w_rows_ref = take(7)
    if chain_root is not None:
        (a_ref,) = take(1)
    cols_ref, rows_ref, lower_ref, top_ref = take(4)
    if later:
        old_cols_ref, old_rows_ref = take(2)
    if chain_root is not None:
        (chain_ref,) = take(1)
    total_ref, summed_ref, gram_ref = take(3)
    sums = take(5)
    rows, cols = lax.axis_size("row"), lax.axis_size("col")
    row, col = lax.axis_index("row"), lax.axis_index("col")
    width = lower_ref.shape[0]
    cyc_cols, cyc_rows = strip_ref.shape[1], raw_rows_ref.shape[0]
    greet("row", "col")
    chain = None
    if chain_root is not None:
        chain = Chain(*chain_root, a_ref, chain_ref, *refs)
        chain.begin()

    if later:
        inverse = inverse_ref[...]
        middle, y_next = get_half(both_ref, 0), get_half(both_ref, 1)
        core = 0.5 * transposed_dot(dot_highest(inverse, middle), inverse)
        z_next = transposed_dot(y_next, inverse) - dot_highest(old_top_ref[...], core)
        finish = side_by_side(jnp.concatenate([inverse.T, -core], axis=0))
        inner = side_by_side(jnp.concatenate([old_top_ref[...].T, z_next.T], axis=0))

    def old_pair(y, w):
        return three_term(split(jnp.concatenate([y, w], axis=1)), finish, dot_f32)

    def correction(z, w):
        return three_term(split(jnp.concatenate([z, w], axis=1)), inner, dot_f32)

    gram_ref[...] = jnp.zeros_like(gram_ref)
    step = min(4, cyc_cols)
    for group in range(cyc_cols // step):
        where = slice(group * step * width, (group + 1) * step * width)
        held = range(group * step, (group + 1) * step)
        tall = jnp.concatenate([strip_ref[:, c, :].T for c in held], axis=0)
        if later:
            w = w_cols_ref[where, :]
            z = old_pair(y_cols_ref[where, :], w)
            old_cols_ref[where, :width] = w
            old_cols_ref[where, width:] = z
            tall = tall - correction(z, w)
        if group * step * cols < first:
            blocks = [
                jnp.where(c * cols + col >= first, tall[i * width : (i + 1) * width], 0.0)
                for i, c in enumerate(held)
            ]
            tall = jnp.concatenate(blocks, axis=0)
        cols_ref[where, :] = tall
        gram_ref[...] += lax.dot_general(
            tall,
            tall,
            (((0,), (0,)), ((), ())),
            precision=lax.Precision.HIGHEST,
            preferred_element_type=jnp.float32,
        )
        if chain is not None and group % 2 == 1:
            chain.serve_turn(group // 2)
    served = (cyc_cols // step) // 2
    put_half(total_ref, 0, gram_ref[...])
    top_at = (first // cols) * width
    holds = col == first % cols
    put_half(total_ref, 1, jnp.where(holds, cols_ref[top_at : top_at + width, :], 0.0))

    def own_rows():
        for group in range(cyc_rows // 4):
            where = slice(group * 4 * width, (group + 1) * 4 * width)
            tall = raw_rows_ref[group * 4 : (group + 1) * 4].reshape(4 * width, width)
            if later:
                w = w_rows_ref[where, :]
                z = old_pair(y_rows_ref[where, :], w)
                old_rows_ref[where, :width] = z
                old_rows_ref[where, width:] = w
                tall = tall - correction(z, w)
            for i in range(4):
                block = tall[i * width : (i + 1) * width]
                at = group * 4 + i
                if at * rows < first:
                    block = jnp.where(at * rows + row >= first, block, 0.0)
                rows_ref[at * width : (at + 1) * width, :] = block
        if chain is not None:
            chain.serve_turn(served)

    sum_over_col(total_ref, summed_ref, *sums, between=own_rows)
    lower_ref[...] = get_half(summed_ref, 0)

    def beside(b):
        if chain is not None:

            @pl.when(b % 2 == 1)
            def _():
                chain.serve_turn(served + 1 + b // 2)

    eliminate(lower_ref, True, beside)
    top_ref[...] = transposed_dot(get_half(summed_ref, 1), lower_ref[...]) - eye(width)
    if chain is not None:

        @pl.loop(served + 1 + width // LEAF // 2, chain.turns())
        def _(turn):
            chain.serve_turn(turn)

        chain.end()


def prepare(strip, raw_rows, first, later, matrix, chain_root, collective_id):
    width, cyc_cols, _ = strip.shape
    cyc_rows = raw_rows.shape[0]
    f32, vmem = jnp.float32, pl.BlockSpec(memory_space=pltpu.VMEM)
    square = jax.ShapeDtypeStruct((width, width), f32)
    args = [strip, raw_rows]
    out_shape = [
        jax.ShapeDtypeStruct((cyc_cols * width, width), f32),
        jax.ShapeDtypeStruct((cyc_rows * width, width), f32),
        square,
        square,
    ]
    if later is not None:
        args += later
        out_shape += [
            jax.ShapeDtypeStruct((cyc_cols * width, 2 * width), f32),
            jax.ShapeDtypeStruct((cyc_rows * width, 2 * width), f32),
        ]
    specs = [vmem] * len(args)
    sums = sum_scratch(width)
    scratch = [sums[0], sums[0], pltpu.VMEM((width, width), f32)] + sums[1:]
    if chain_root is not None:
        args.append(matrix)
        specs.append(pl.BlockSpec(memory_space=pl.ANY))
        out_shape.append(jax.ShapeDtypeStruct((cyc_rows, width, width), f32))
        scratch += chain_sems(cyc_rows)
    return pl.pallas_call(
        functools.partial(prepare_kernel, first, later is not None, chain_root),
        out_shape=out_shape,
        in_specs=specs,
        out_specs=[vmem] * len(out_shape),
        scratch_shapes=scratch,
        compiler_params=remote_params(collective_id),
    )(*args)


def panel_kernel(first, group, mirrors, later, root_strip, *refs):
    refs = list(refs)
    take = lambda n: [refs.pop(0) for _ in range(n)]
    a_ref, cols_ref, lower_ref, top_ref, own_ref = take(5)
    if later:
        old_cols_ref, old_rows_ref = take(2)
    if root_strip is not None:
        (strip_ref,) = take(1)
    w_ref, inverse_ref, rows_ref, spread_ref, w_rows_ref, both_ref = take(6)
    if root_strip is not None:
        (strip_out,) = take(1)
    held, weights, part, arrived, sems = take(5)
    sum_send, sum_recv, on_send, on_recv, tree_send, tree_recv, local_sem = take(7)
    total_ref, *sums = take(6)
    if later:
        small_ref, old_weights = take(2)
    rows, cols = lax.axis_size("row"), lax.axis_size("col")
    row, col = lax.axis_index("row"), lax.axis_index("col")
    cyc_cols, width = a_ref.shape[1:]
    pieces, tile = part.shape[1:3]
    tiles = cols * pieces
    greet("row", "col")

    def owner(index):
        return (col + 1 + index // pieces) % cols

    def fetch(index, slot):
        start = (owner(index) * pieces + index % pieces) * tile
        return [
            pltpu.make_async_copy(
                a_ref.at[pl.ds(pl.multiple_of(start, tile), tile), c, :],
                held.at[slot, c],
                sems.at[slot, c],
            )
            for c in range(cyc_cols)
        ]

    for copy in fetch(0, 0):
        copy.start()
    strip = None
    if root_strip is not None:
        root, layer = root_strip
        strip = Strip(root, strip_ref.at[layer], strip_out, *refs)
        strip.begin()

    square_row = lax.broadcasted_iota(jnp.int32, (width, width), 0)
    square_lane = lax.broadcasted_iota(jnp.int32, (width, width), 1)
    identity = (square_row == square_lane).astype(jnp.float32)
    if later:
        small_ref[...] = jnp.zeros_like(small_ref)

    tall = min(4, cyc_cols)

    @pl.loop(0, cyc_cols // tall)
    def _(chunk):
        where = pl.ds(pl.multiple_of(chunk * tall * width, tall * width), tall * width)
        w = transposed_dot(cols_ref[where, :], lower_ref[...])
        units = [
            identity * flag((chunk * tall + c) * cols + col == first) for c in range(tall)
        ]
        w = w - jnp.concatenate(units, axis=0)
        w_ref[where, :] = w
        both = side_by_side(w)
        weights[where, :] = both
        if later:
            small_ref[...] += three_term(split(old_cols_ref[where, :]), both, transposed_left)

    if later:
        high, low = split(small_ref[...])
        old_weights[:, :width] = high
        old_weights[:, width:] = low

    def to_owner(index):
        q, piece = owner(index), index % pieces
        return remote(
            part.at[q, piece],
            arrived.at[index // pieces, piece],
            sum_send.at[index],
            sum_recv.at[index],
            col=q,
        )

    @pl.loop(0, tiles)
    def _(index):
        slot = lax.rem(index, 2)

        @pl.when(index + 1 < tiles)
        def _():
            for copy in fetch(index + 1, 1 - slot):
                copy.start()

        for copy in fetch(index, slot):
            copy.wait()
        total = None
        for chunk in range(cyc_cols // group):
            parts = [split(held[slot, chunk * group + g]) for g in range(group)]
            left = tuple(jnp.concatenate([p[i] for p in parts], axis=1) for i in range(2))
            right = weights[chunk * group * width : (chunk + 1) * group * width, :]
            term = three_term(left, right, dot_f32)
            total = term if total is None else total + term
        q, piece = owner(index), index % pieces
        if later:
            start = pl.multiple_of((q * pieces + piece) * tile, tile)
            old = split(old_rows_ref[pl.ds(start, tile), :])
            total = total - three_term(old, old_weights[...], dot_f32)
        part[q, piece] = total

        @pl.when(index < tiles - pieces)
        def _():
            to_owner(index).start()

        if strip is not None:
            strip.serve_turn(index)

    if strip is not None:

        @pl.loop(tiles, max(tiles, strip.turns()))
        def _(turn):
            strip.serve_turn(turn)

    inverse_ref[...] = -top_ref[...]
    eliminate(inverse_ref, False)
    for chunk in range(own_ref.shape[0] // (4 * width)):
        where = slice(chunk * 4 * width, (chunk + 1) * 4 * width)
        w = transposed_dot(own_ref[where, :], lower_ref[...])
        units = [identity * flag((chunk * 4 + i) * rows + row == first) for i in range(4)]
        w_rows_ref[where, :] = w - jnp.concatenate(units, axis=0)

    bits = rows.bit_length() - 1
    order = list(range(1, bits)) + [0]
    across = [row + (1 - 2 * ((row // 2**b) % 2)) * 2**b for b in order]

    def spot(mirror, q, piece):
        start = (q * pieces + piece) * tile
        if tile >= width:
            blocks = tile // width
            return spread_ref.at[pl.ds((q * pieces + piece) * blocks, blocks), mirror]
        inside = pl.ds(pl.multiple_of(start % width, tile), tile)
        return spread_ref.at[start // width, mirror, inside]

    def source(q, piece):
        view = rows_ref.at[q, piece]
        return view.reshape(tile // width, width, width) if tile >= width else view

    def onward(q, piece, side):
        return remote(
            rows_ref.at[q, piece],
            rows_ref.at[q, piece],
            on_send.at[side, q, piece],
            on_recv.at[q, piece],
            col=(col + 1 - 2 * side + cols) % cols,
        )

    def branch(mirror, q, piece, t, view):
        return remote(
            view,
            spot(mirror, q, piece),
            tree_send.at[mirror, q, piece, t],
            tree_recv.at[mirror, q, piece],
            row=across[t],
        )

    def own_copy(mirror, q, piece):
        return pltpu.make_async_copy(
            source(q, piece), spot(mirror, q, piece), local_sem.at[mirror, q, piece]
        )

    below = []
    for mirror in range(mirrors):
        root = col + mirror * cols
        differ = [((row // 2**b) % 2 + (root // 2**b) % 2) % 2 for b in order]
        below.append([sum(differ[t:]) for t in range(bits)])

    def root_start(q, piece):
        for mirror in range(mirrors):

            @pl.when(below[mirror][0] == 0)
            def _():
                own_copy(mirror, q, piece).start()
                for t in range(bits):
                    branch(mirror, q, piece, t, source(q, piece)).start()

    def relay(mirror, q, piece):
        for t in range(bits):
            copy = branch(mirror, q, piece, t, spot(mirror, q, piece))
            if t == 0:
                copy.wait_recv()

            @pl.when(below[mirror][t] == 0)
            def _():
                copy.start()

    @pl.loop(0, pieces)
    def _(piece):
        value = part[col, piece]
        for step in range(cols - 1):
            to_owner(step * pieces + piece).wait_recv()
            value = value + arrived[step, piece]
        rows_ref[col, piece] = value
        for side in range(2):

            @pl.when((col < cols - 1) if side == 0 else (col > 0))
            def _():
                onward(col, piece, side).start()

    both_sides = jnp.minimum(col, cols - 1 - col)
    longer = jnp.where(2 * col < cols - 1, 1, -1)

    def visit(number):
        group, piece = number // pieces, number % pieces
        paired = group <= 2 * both_sides
        far = jnp.where(paired, (group + 1) // 2, group - both_sides)
        way = jnp.where(paired, 1 - 2 * (group % 2), longer)
        return col + far * way, piece, way

    visits = cols * pieces
    lags = [LAG * below[mirror][0] for mirror in range(mirrors)]

    @pl.loop(0, visits + LAG * bits)
    def _(number):
        q, piece, way = visit(number)

        @pl.when(number < visits)
        def _():
            for side in range(2):

                @pl.when((number >= pieces) & (way == 1 - 2 * (1 - side)))
                def _():
                    copy = onward(q, piece, side)
                    copy.wait_recv()

                    @pl.when((col < cols - 1) if side == 0 else (col > 0))
                    def _():
                        copy.start()

            root_start(q, piece)

        for mirror in range(mirrors):
            late = number - lags[mirror]

            @pl.when((below[mirror][0] != 0) & (late >= 0) & (late < visits))
            def _():
                q, piece, _way = visit(late)
                relay(mirror, q, piece)

    @pl.loop(0, cols)
    def _(q):
        @pl.loop(0, pieces)
        def _(piece):
            @pl.when((q <= col) & (col < cols - 1))
            def _():
                onward(q, piece, 0).wait_send()

            @pl.when((q >= col) & (col > 0))
            def _():
                onward(q, piece, 1).wait_send()

            for mirror in range(mirrors):

                @pl.when(below[mirror][0] == 0)
                def _():
                    own_copy(mirror, q, piece).wait()

                for t in range(bits):

                    @pl.when(below[mirror][t] == 0)
                    def _():
                        branch(mirror, q, piece, t, spot(mirror, q, piece)).wait_send()

    @pl.loop(0, tiles - pieces)
    def _(index):
        to_owner(index).wait_send()

    small = jnp.zeros((width, width), jnp.float32)
    for chunk in range(cyc_cols // tall):
        where = slice(chunk * tall * width, (chunk + 1) * tall * width)
        y = spread_ref[chunk * tall // mirrors : (chunk + 1) * tall // mirrors]
        y = y.reshape(tall * width, width)
        small = small + three_term(split(y), weights[where, :], transposed_left)
    put_half(total_ref, 0, small.T)
    c = first // cols
    y = spread_ref[c // mirrors, c % mirrors]
    put_half(total_ref, 1, jnp.where(col == first % cols, y, 0.0))
    sum_over_col(total_ref, both_ref, *sums)

    if strip is not None:
        strip.end()


def panel_product(matrix, cols, lower, w_top, own, first, old, root_strip, collective_id):
    rows_size, cols_size = lax.axis_size("row"), lax.axis_size("col")
    mirrors = rows_size // cols_size
    bits = rows_size.bit_length() - 1
    cyc_rows, width, cyc_cols, _ = matrix.shape
    n_rows = cyc_rows * width
    depth = n_rows // cols_size
    tile = min(256, depth)
    pieces = depth // tile
    flat = matrix.reshape(n_rows, cyc_cols, width)
    vmem, anywhere = pl.BlockSpec(memory_space=pltpu.VMEM), pl.BlockSpec(memory_space=pl.ANY)
    f32, dma = jnp.float32, pltpu.SemaphoreType.DMA
    args, specs = [flat, cols, lower, w_top, own], [anywhere, vmem, vmem, vmem, vmem]
    if old is not None:
        args += list(old)
        specs += [vmem, vmem]
    out_shape = [
        jax.ShapeDtypeStruct(cols.shape, f32),
        jax.ShapeDtypeStruct((width, width), f32),
        jax.ShapeDtypeStruct((cols_size, pieces, tile, width), f32),
        jax.ShapeDtypeStruct((cyc_rows, mirrors, width, width), f32),
        jax.ShapeDtypeStruct((n_rows, width), f32),
        jax.ShapeDtypeStruct((rows_size, 2 * width // rows_size, width), f32),
    ]
    scratch = [
        pltpu.VMEM((2, cyc_cols, tile, width), f32),
        pltpu.VMEM((cols.shape[0], 2 * width), jnp.bfloat16),
        pltpu.VMEM((cols_size, pieces, tile, width), f32),
        pltpu.VMEM((cols_size - 1, pieces, tile, width), f32),
        dma((2, cyc_cols)),
        dma((cols_size * pieces,)),
        dma((cols_size * pieces,)),
        dma((2, cols_size, pieces)),
        dma((cols_size, pieces)),
        dma((mirrors, cols_size, pieces, bits)),
        dma((mirrors, cols_size, pieces)),
        dma((mirrors, cols_size, pieces)),
    ] + sum_scratch(width)
    if old is not None:
        scratch += [
            pltpu.VMEM((2 * width, width), f32),
            pltpu.VMEM((2 * width, 2 * width), jnp.bfloat16),
        ]
    if root_strip is not None:
        args.append(matrix)
        specs.append(anywhere)
        out_shape.append(jax.ShapeDtypeStruct(matrix.shape[1:], f32))
        scratch += STRIP_SEMS
    return pl.pallas_call(
        functools.partial(
            panel_kernel, first, min(8, cyc_cols), mirrors, old is not None, root_strip
        ),
        out_shape=out_shape,
        in_specs=specs,
        out_specs=[vmem] * len(out_shape),
        scratch_shapes=scratch,
        compiler_params=remote_params(collective_id),
    )(*args)


def update_kernel(
    group, a_ref, uh_ref, ul_ref, vh_ref, vl_ref, out_ref, held, done, sems, out_sems
):
    tile = uh_ref.shape[0]
    cyc_cols, width = a_ref.shape[1:]
    step, steps = pl.program_id(0), pl.num_programs(0)
    slot, copies = fetch_tiles(a_ref, held, sems, tile)
    high, low = uh_ref[...], ul_ref[...]

    def stores(index, where):
        return [
            pltpu.make_async_copy(
                done.at[where, c],
                out_ref.at[pl.ds(index * tile, tile), c, :],
                out_sems.at[where, c],
            )
            for c in range(cyc_cols)
        ]

    @pl.when(step >= 2)
    def _():
        for copy in stores(step - 2, slot):
            copy.wait()

    for copy in copies:
        copy.wait()
    started = stores(step, slot)
    for chunk in range(cyc_cols // group):
        columns = slice(chunk * group * width, (chunk + 1) * group * width)
        v_high, v_low = vh_ref[:, columns], vl_ref[:, columns]
        delta = dot_f32(high, v_low) + dot_f32(low, v_high) + dot_f32(high, v_high)
        for g in range(group):
            c = chunk * group + g
            done[slot, c] = held[slot, c] - delta[:, g * width : (g + 1) * width]
            started[c].start()

    @pl.when(step == steps - 1)
    def _():
        for copy in stores(step, slot):
            copy.wait()

        @pl.when(steps > 1)
        def _():
            for copy in stores(step - 1, 1 - slot):
                copy.wait()


def finish_kernel(
    both_ref, inverse_ref, y_cols_ref, w_cols_ref, y_rows_ref, w_rows_ref,
    old_cols_ref, old_rows_ref, lh_ref, ll_ref, rh_ref, rl_ref,
):
    width = inverse_ref.shape[0]
    inverse = inverse_ref[...]
    core = 0.5 * transposed_dot(dot_highest(inverse, get_half(both_ref, 0)), inverse)
    finish = side_by_side(jnp.concatenate([inverse.T, -core], axis=0))
    step = 4 * width

    @pl.loop(0, y_rows_ref.shape[0] // step)
    def _(group):
        where = pl.ds(pl.multiple_of(group * step, step), step)
        w = w_rows_ref[where, :]
        z = three_term(
            split(jnp.concatenate([y_rows_ref[where, :], w], axis=1)), finish, dot_f32
        )
        for at, value in ((0, old_rows_ref[where, :]), (2 * width, z), (3 * width, w)):
            high, low = split(value)
            lh_ref[where, at : at + value.shape[1]] = high
            ll_ref[where, at : at + value.shape[1]] = low

    @pl.loop(0, y_cols_ref.shape[0] // step)
    def _(group):
        where = pl.ds(pl.multiple_of(group * step, step), step)
        w = w_cols_ref[where, :]
        z = three_term(
            split(jnp.concatenate([y_cols_ref[where, :], w], axis=1)), finish, dot_f32
        )
        for at, value in ((0, old_cols_ref[where, :]), (2 * width, w), (3 * width, z)):
            high, low = split(value.T)
            rh_ref[at : at + value.shape[1], where] = high
            rl_ref[at : at + value.shape[1], where] = low


def finish_factors(both, inverse, y_cols, w_cols, y_rows, w_rows, old_cols, old_rows):
    width = inverse.shape[0]
    left = jax.ShapeDtypeStruct((y_rows.shape[0], 4 * width), jnp.bfloat16)
    right = jax.ShapeDtypeStruct((4 * width, y_cols.shape[0]), jnp.bfloat16)
    return pl.pallas_call(
        finish_kernel,
        out_shape=[left, left, right, right],
        compiler_params=pltpu.CompilerParams(vmem_limit_bytes=VMEM_LIMIT),
    )(both, inverse, y_cols, w_cols, y_rows, w_rows, old_cols, old_rows)


def apply_update(matrix, left_high, left_low, high, low):
    cyc_rows, width, cyc_cols, _ = matrix.shape
    n_rows, depth = left_high.shape
    tile = min(256, n_rows)
    whole = pl.BlockSpec(high.shape, lambda i: (0, 0), pipeline_mode=pl.Buffered(1))
    some = pl.BlockSpec((tile, depth), lambda i: (i, 0))
    held = pltpu.VMEM((2, cyc_cols, tile, width), jnp.float32)
    sems = pltpu.SemaphoreType.DMA((2, cyc_cols))
    return pl.pallas_call(
        functools.partial(update_kernel, min(4, cyc_cols)),
        grid=(n_rows // tile,),
        out_shape=jax.ShapeDtypeStruct((n_rows, cyc_cols, width), jnp.float32),
        in_specs=[pl.BlockSpec(memory_space=pl.ANY), some, some, whole, whole],
        out_specs=pl.BlockSpec(memory_space=pl.ANY),
        scratch_shapes=[held, held, sems, sems],
        compiler_params=pltpu.CompilerParams(vmem_limit_bytes=VMEM_LIMIT),
    )(matrix.reshape(n_rows, cyc_cols, width), left_high, left_low, high, low)


def local(matrix):
    row_count = lax.axis_size("row")
    col_count = lax.axis_size("col")
    cyc_rows, width, cyc_cols, _ = matrix.shape
    n_rows, n_cols = cyc_rows * width, cyc_cols * width

    strip, raw = spread(matrix, 0, 0, 0, 0, 0)
    cols, own, lower, w_top, raw = prepare(
        strip, raw, 1, None, matrix, (1 % col_count, 1 // col_count), 1
    )
    strip_of = (1 % row_count, 1 // row_count)
    wc, inverse, y_rows, y_cols, wr, both, strip = panel_product(
        matrix, cols, lower, w_top, own, 1, None, strip_of, 2
    )
    later = [
        both,
        inverse,
        w_top,
        y_cols.reshape(n_cols, width),
        wc,
        y_rows.reshape(n_rows, width),
        wr,
    ]
    cols, own, lower, w_top, old_cols, old_rows = prepare(strip, raw, 2, later, matrix, None, 3)
    wc, inverse, y_rows, y_cols, wr_last, both = panel_product(
        matrix, cols, lower, w_top, own, 2, (old_cols, old_rows), None, 4
    )
    y_rows, y_cols = y_rows.reshape(n_rows, width), y_cols.reshape(n_cols, width)
    factors = finish_factors(both, inverse, y_cols, wc, y_rows, wr_last, old_cols, old_rows)
    reduced = apply_update(matrix, *factors).reshape(matrix.shape)
    bases = jnp.concatenate([wr, wr_last], axis=1).reshape(cyc_rows, width, PANELS * width)
    return (reduced, bases)


def solution(mesh):
    return jax.shard_map(
        local,
        mesh=mesh,
        in_specs=(P(None, "row", None, "col"),),
        out_specs=(P(None, "row", None, "col"), P(None, "row", None)),
        check_vma=False,
    )
```

```python
import functools

import jax
import jax.numpy as jnp
from jax import lax
from jax.experimental import pallas as pl
from jax.experimental.pallas import tpu as pltpu
from jax.sharding import PartitionSpec as P

PANELS = 2
MESH = pl.DeviceIdType.MESH
VMEM_LIMIT = 60 * 1024 * 1024


def dot_highest(left, right):
    return jnp.dot(left, right, precision=lax.Precision.HIGHEST, preferred_element_type=jnp.float32)


def greet(*axes):
    barrier = pltpu.get_barrier_semaphore()
    total = 0
    for axis in axes:
        me, size = lax.axis_index(axis), lax.axis_size(axis)
        for step in range(1, size):
            pl.semaphore_signal(
                barrier, inc=1, device_id={axis: lax.rem(me + step, size)}, device_id_type=MESH
            )
        total += size - 1
    pl.semaphore_wait(barrier, total)


def remote(src, dst, send_sem, recv_sem, **device):
    return pltpu.make_async_remote_copy(
        src_ref=src,
        dst_ref=dst,
        send_sem=send_sem,
        recv_sem=recv_sem,
        device_id=device,
        device_id_type=MESH,
    )


def remote_params(collective_id):
    return pltpu.CompilerParams(
        collective_id=collective_id, has_side_effects=True, vmem_limit_bytes=VMEM_LIMIT
    )

STREAM_CHUNKS = 8

LAG = 2


def ring_place(pair, pairs):
    return pair + (pair // 2) * (1 - 2 * (pair % 2)) if pairs == 4 else pair


class Strip:
    def __init__(self, root, strip_ref, out_ref, ring_send, pair_send, recv, local_sem):
        size = lax.axis_size("row")
        me = lax.axis_index("row")
        pairs = size // 2
        pair, core = me // 2, me % 2
        place = ring_place(pair, pairs)
        distance = (place - ring_place(root // 2, pairs) + pairs) % pairs
        stream = (core + root % 2) % 2
        hop = (distance * (1 - 2 * stream) + stream * pairs) % pairs
        self.target = 2 * ring_place((place + 1 - 2 * stream + pairs) % pairs, pairs) + core
        self.sibling = 2 * pair + 1 - core
        self.root, self.me, self.pairs = root, me, pairs
        self.stream, self.hop, self.distance = stream, hop, distance
        self.strip_ref, self.out_ref = strip_ref, out_ref
        self.ring_send, self.pair_send = ring_send, pair_send
        self.recv, self.local_sem = recv, local_sem
        self.piece = out_ref.shape[0] // (2 * STREAM_CHUNKS)

    def rows_of(self, which, i):
        start = (which * STREAM_CHUNKS + i) * self.piece
        return pl.ds(pl.multiple_of(start, self.piece), self.piece)

    def to_ring(self, i, source, which):
        rows = self.rows_of(which, i)
        return remote(
            source.at[rows],
            self.out_ref.at[rows],
            self.ring_send.at[i],
            self.recv.at[which, i],
            row=self.target,
        )

    def to_sibling(self, i, source, which, slot):
        rows = self.rows_of(which, i)
        return remote(
            source.at[rows],
            self.out_ref.at[rows],
            self.pair_send.at[slot, i],
            self.recv.at[which, i],
            row=self.sibling,
        )

    def root_copies(self):
        copies = []
        for i in range(STREAM_CHUNKS):
            copies.append(self.to_ring(i, self.strip_ref, 0))
            copies.append(self.to_sibling(i, self.strip_ref, 1, 1))
        for i in range(STREAM_CHUNKS):
            copies.append(self.to_sibling(i, self.strip_ref, 0, 0))
        return copies

    def begin(self):
        @pl.when(self.me == self.root)
        def _():
            for copy in self.root_copies():
                copy.start()
            pltpu.make_async_copy(self.strip_ref, self.out_ref, self.local_sem).start()

    def serve(self, i):
        onward = self.to_ring(i, self.out_ref, self.stream)
        onward.wait_recv()

        @pl.when(self.hop < self.pairs - 1)
        def _():
            onward.start()

        @pl.when(self.distance > 0)
        def _():
            self.to_sibling(i, self.out_ref, self.stream, 0).start()

    def serve_turn(self, turn):
        first = 2 * (turn - 2 * self.hop)
        for half in range(2):
            i = first + half

            @pl.when((self.me != self.root) & (i >= 0) & (i < STREAM_CHUNKS))
            def _():
                self.serve(i)

    def turns(self):
        return STREAM_CHUNKS // 2 + 2 * (self.pairs - 1)

    def end(self):
        @pl.when(self.me == self.root)
        def _():
            for copy in self.root_copies():
                copy.wait_send()
            pltpu.make_async_copy(self.strip_ref, self.out_ref, self.local_sem).wait()

        @pl.when(self.me != self.root)
        def _():
            for i in range(STREAM_CHUNKS):
                self.to_ring(i, self.out_ref, 1 - self.stream).wait_recv()

                @pl.when(self.hop < self.pairs - 1)
                def _():
                    self.to_ring(i, self.out_ref, self.stream).wait_send()

                @pl.when(self.distance > 0)
                def _():
                    self.to_sibling(i, self.out_ref, self.stream, 0).wait_send()


STRIP_SEMS = [
    pltpu.SemaphoreType.DMA((STREAM_CHUNKS,)),
    pltpu.SemaphoreType.DMA((2, STREAM_CHUNKS)),
    pltpu.SemaphoreType.DMA((2, STREAM_CHUNKS)),
    pltpu.SemaphoreType.DMA,
]


class Chain:
    def __init__(self, root, layer, a_ref, out_ref, send, recv, local_sems):
        self.col, self.cols = lax.axis_index("col"), lax.axis_size("col")
        self.root, self.layer, self.a_ref, self.out_ref = root, layer, a_ref, out_ref
        self.send, self.recv, self.local_sems = send, recv, local_sems
        self.count = recv.shape[0]
        self.piece = out_ref.shape[0] // self.count
        self.ways = [(self.col >= root) & (self.col < self.cols - 1), (self.col <= root) & (self.col > 0)]

    def part(self, i):
        return pl.ds(pl.multiple_of(i * self.piece, self.piece), self.piece)

    def local(self, i):
        return pltpu.make_async_copy(
            self.a_ref.at[self.part(i), :, self.layer, :],
            self.out_ref.at[self.part(i)],
            self.local_sems.at[i],
        )

    def onward(self, i, side):
        view = self.out_ref.at[self.part(i)]
        target = (self.col + 1 - 2 * side + self.cols) % self.cols
        return remote(view, view, self.send.at[side, i], self.recv.at[i], col=target)

    def begin(self):
        @pl.when(self.col == self.root)
        def _():
            for i in range(self.count):
                self.local(i).start()

    def serve(self, i):
        @pl.when(self.col == self.root)
        def _():
            self.local(i).wait()

        @pl.when(self.col != self.root)
        def _():
            self.onward(i, 0).wait_recv()

        for side in range(2):

            @pl.when(self.ways[side])
            def _():
                self.onward(i, side).start()

    def serve_turn(self, turn):
        far = jnp.maximum(self.col - self.root, self.root - self.col)
        i = turn - far

        @pl.when((i >= 0) & (i < self.count))
        def _():
            self.serve(i)

    def turns(self):
        return self.count + self.cols

    def end(self):
        for i in range(self.count):
            for side in range(2):

                @pl.when(self.ways[side])
                def _():
                    self.onward(i, side).wait_send()


def chain_sems(cyc_rows):
    count = min(8, cyc_rows)
    dma = pltpu.SemaphoreType.DMA
    return [dma((2, count)), dma((count,)), dma((count,))]


def spread_kernel(root, layer, col_root, col_layer, a_ref, strip_ref, rows_ref, *sems):
    greet("row", "col")
    strip = Strip(root, a_ref.at[layer], strip_ref, *sems[: len(STRIP_SEMS)])
    chain = Chain(col_root, col_layer, a_ref, rows_ref, *sems[len(STRIP_SEMS) :])
    strip.begin()
    chain.begin()

    @pl.loop(0, max(strip.turns(), chain.turns()))
    def _(turn):
        chain.serve_turn(turn)
        strip.serve_turn(turn)

    strip.end()
    chain.end()


def spread(matrix, root, layer, col_root, col_layer, collective_id):
    cyc_rows, width, _, _ = matrix.shape
    return pl.pallas_call(
        functools.partial(spread_kernel, root, layer, col_root, col_layer),
        out_shape=[
            jax.ShapeDtypeStruct(matrix.shape[1:], matrix.dtype),
            jax.ShapeDtypeStruct((cyc_rows, width, width), matrix.dtype),
        ],
        in_specs=[pl.BlockSpec(memory_space=pl.ANY)],
        out_specs=[pl.BlockSpec(memory_space=pltpu.VMEM)] * 2,
        scratch_shapes=STRIP_SEMS + chain_sems(cyc_rows),
        compiler_params=remote_params(collective_id),
    )(matrix)


def sum_over_col(x_ref, out_ref, held, col_send, col_recv, row_send, row_recv, between=None):
    rows, cols = lax.axis_size("row"), lax.axis_size("col")
    row, col = lax.axis_index("row"), lax.axis_index("col")
    copies = []
    for step in range(1, cols):
        copy = remote(
            x_ref.at[row],
            held.at[col],
            col_send.at[step],
            col_recv.at[step],
            col=lax.rem(col + step, cols),
        )
        copy.start()
        copies.append(copy)
    held[col] = x_ref[row]
    for copy in copies:
        copy.wait()
    value = held[0]
    for q in range(1, cols):
        value = value + held[q]
    out_ref[row] = value
    copies = []
    for step in range(1, rows):
        copy = remote(
            out_ref.at[row],
            out_ref.at[row],
            row_send.at[step],
            row_recv.at[step],
            row=lax.rem(row + step, rows),
        )
        copy.start()
        copies.append(copy)
    if between is not None:
        between()
    for copy in copies:
        copy.wait()


def sum_scratch(width):
    rows, cols = lax.axis_size("row"), lax.axis_size("col")
    piece = 2 * width // rows
    dma = pltpu.SemaphoreType.DMA
    return [
        pltpu.VMEM((rows, piece, width), jnp.float32),
        pltpu.VMEM((cols, piece, width), jnp.float32),
        dma((cols,)),
        dma((cols,)),
        dma((rows,)),
        dma((rows,)),
    ]


def put_half(x_ref, half, value):
    rows, piece, width = x_ref.shape
    for r in range(rows // 2):
        x_ref[half * (rows // 2) + r] = value[r * piece : (r + 1) * piece]


def get_half(x_ref, half):
    rows, piece, width = x_ref.shape
    return x_ref[pl.ds(half * (rows // 2), rows // 2)].reshape(width, width)


LEAF = 16


def eliminate(ref, symmetric, beside=None):
    size = ref.shape[0]
    strip_row = lax.broadcasted_iota(jnp.int32, (LEAF, size), 0)
    strip_lane = lax.broadcasted_iota(jnp.int32, (LEAF, size), 1)
    row = lax.broadcasted_iota(jnp.int32, (size, size), 0)
    lane = lax.broadcasted_iota(jnp.int32, (size, size), 1)

    def block(b, carry):
        start = pl.multiple_of(b * LEAF, LEAF)
        whole = ref[...]
        strip = ref[pl.ds(start, LEAF), :]
        columns = [jnp.broadcast_to(strip[:, i : i + 1], (LEAF, size)) for i in range(LEAF)]
        panel = jnp.where(strip_lane < LEAF, (strip_row == strip_lane).astype(jnp.float32), strip)
        for i in range(LEAF):
            column = columns[i]
            pivot = jnp.broadcast_to(column[i : i + 1, :], (LEAF, size))
            if symmetric:
                scale = lax.rsqrt(pivot)
                scale = scale * (1.5 - 0.5 * pivot * scale * scale)
                column = column * scale
                touched = strip_row > i
            else:
                scale = 1.0 / pivot
                touched = strip_row != i

            def step(x):
                lead = jnp.broadcast_to(x[i : i + 1, :], (LEAF, size)) * scale
                return jnp.where(touched, x - column * lead, jnp.where(strip_row == i, lead, x))

            panel = step(panel)
            for j in range(i + 1, LEAF):
                columns[j] = step(columns[j])
        base = jnp.where(lane < LEAF, 0.0, whole)
        if symmetric:
            factor = jnp.where((strip_lane >= LEAF) & (strip_lane < size - start), panel, 0.0)
            factor = pltpu.roll(factor, start, axis=1)
            change = lax.dot_general(
                factor,
                panel,
                (((0,), (0,)), ((), ())),
                precision=lax.Precision.HIGHEST,
                preferred_element_type=jnp.float32,
            )
            ref[...] = jnp.where(row < start, whole, base - change)
        else:
            inside = (row >= start) & (row < start + LEAF)
            factor = jnp.where(inside | (lane >= LEAF), 0.0, whole)
            padded = jnp.concatenate([panel, jnp.zeros((size - LEAF, size), jnp.float32)], axis=0)
            ref[...] = base - dot_highest(factor, padded)
        ref[pl.ds(start, LEAF), :] = panel
        ref[...] = pltpu.roll(ref[...], size - LEAF, axis=1)
        if beside is not None:
            beside(b)
        return carry

    lax.fori_loop(0, size // LEAF, block, 0)
    if symmetric:
        ref[...] = jnp.where(row >= lane, ref[...], 0.0)


def transposed_dot(left, right):
    return lax.dot_general(
        left,
        right,
        (((1,), (1,)), ((), ())),
        precision=lax.Precision.HIGHEST,
        preferred_element_type=jnp.float32,
    )


def split(value):
    high = value.astype(jnp.bfloat16)
    return high, (value - high.astype(jnp.float32)).astype(jnp.bfloat16)


def dot_f32(left, right):
    return jnp.dot(left, right, preferred_element_type=jnp.float32)


def tile_copies(a_ref, held, sems, tile, index, slot):
    return [
        pltpu.make_async_copy(
            a_ref.at[pl.ds(index * tile, tile), c, :], held.at[slot, c], sems.at[slot, c]
        )
        for c in range(a_ref.shape[1])
    ]


def fetch_tiles(a_ref, held, sems, tile):
    step, steps = pl.program_id(0), pl.num_programs(0)
    slot = lax.rem(step, 2)

    @pl.when(step == 0)
    def _():
        for copy in tile_copies(a_ref, held, sems, tile, step, slot):
            copy.start()

    @pl.when(step + 1 < steps)
    def _():
        for copy in tile_copies(a_ref, held, sems, tile, step + 1, 1 - slot):
            copy.start()

    return slot, tile_copies(a_ref, held, sems, tile, step, slot)


def transposed_left(left, right):
    return lax.dot_general(
        left, right, (((0,), (0,)), ((), ())), preferred_element_type=jnp.float32
    )


def three_term(left, right, dot):
    high, low = left
    width = right.shape[1] // 2
    wide = dot(high, right)
    return wide[:, width:] + dot(low, right[:, :width]) + wide[:, :width]


def eye(width):
    row = lax.broadcasted_iota(jnp.int32, (width, width), 0)
    lane = lax.broadcasted_iota(jnp.int32, (width, width), 1)
    return (row == lane).astype(jnp.float32)


def flag(condition):
    return condition.astype(jnp.float32)


def side_by_side(value):
    return jnp.concatenate(split(value), axis=1)


def prepare_kernel(first, later, chain_root, *refs):
    refs = list(refs)
    take = lambda n: [refs.pop(0) for _ in range(n)]
    strip_ref, raw_rows_ref = take(2)
    if later:
        both_ref, inverse_ref, old_top_ref, y_cols_ref, w_cols_ref, y_rows_ref, w_rows_ref = take(7)
    if chain_root is not None:
        (a_ref,) = take(1)
    cols_ref, rows_ref, lower_ref, top_ref = take(4)
    if later:
        old_cols_ref, old_rows_ref = take(2)
    if chain_root is not None:
        (chain_ref,) = take(1)
    total_ref, summed_ref, gram_ref = take(3)
    sums = take(5)
    rows, cols = lax.axis_size("row"), lax.axis_size("col")
    row, col = lax.axis_index("row"), lax.axis_index("col")
    width = lower_ref.shape[0]
    cyc_cols, cyc_rows = strip_ref.shape[1], raw_rows_ref.shape[0]
    greet("row", "col")
    chain = None
    if chain_root is not None:
        chain = Chain(*chain_root, a_ref, chain_ref, *refs)
        chain.begin()

    if later:
        inverse = inverse_ref[...]
        middle, y_next = get_half(both_ref, 0), get_half(both_ref, 1)
        core = 0.5 * transposed_dot(dot_highest(inverse, middle), inverse)
        z_next = transposed_dot(y_next, inverse) - dot_highest(old_top_ref[...], core)
        finish = side_by_side(jnp.concatenate([inverse.T, -core], axis=0))
        inner = side_by_side(jnp.concatenate([old_top_ref[...].T, z_next.T], axis=0))

    def old_pair(y, w):
        return three_term(split(jnp.concatenate([y, w], axis=1)), finish, dot_f32)

    def correction(z, w):
        return three_term(split(jnp.concatenate([z, w], axis=1)), inner, dot_f32)

    gram_ref[...] = jnp.zeros_like(gram_ref)
    step = min(4, cyc_cols)
    for group in range(cyc_cols // step):
        where = slice(group * step * width, (group + 1) * step * width)
        held = range(group * step, (group + 1) * step)
        tall = jnp.concatenate([strip_ref[:, c, :].T for c in held], axis=0)
        if later:
            w = w_cols_ref[where, :]
            z = old_pair(y_cols_ref[where, :], w)
            old_cols_ref[where, :width] = w
            old_cols_ref[where, width:] = z
            tall = tall - correction(z, w)
        if group * step * cols < first:
            blocks = [
                jnp.where(c * cols + col >= first, tall[i * width : (i + 1) * width], 0.0)
                for i, c in enumerate(held)
            ]
            tall = jnp.concatenate(blocks, axis=0)
        cols_ref[where, :] = tall
        gram_ref[...] += lax.dot_general(
            tall,
            tall,
            (((0,), (0,)), ((), ())),
            precision=lax.Precision.HIGHEST,
            preferred_element_type=jnp.float32,
        )
        if chain is not None and group % 2 == 1:
            chain.serve_turn(group // 2)
    served = (cyc_cols // step) // 2
    put_half(total_ref, 0, gram_ref[...])
    top_at = (first // cols) * width
    holds = col == first % cols
    put_half(total_ref, 1, jnp.where(holds, cols_ref[top_at : top_at + width, :], 0.0))

    def own_rows():
        for group in range(cyc_rows // 4):
            where = slice(group * 4 * width, (group + 1) * 4 * width)
            tall = raw_rows_ref[group * 4 : (group + 1) * 4].reshape(4 * width, width)
            if later:
                w = w_rows_ref[where, :]
                z = old_pair(y_rows_ref[where, :], w)
                old_rows_ref[where, :width] = z
                old_rows_ref[where, width:] = w
                tall = tall - correction(z, w)
            for i in range(4):
                block = tall[i * width : (i + 1) * width]
                at = group * 4 + i
                if at * rows < first:
                    block = jnp.where(at * rows + row >= first, block, 0.0)
                rows_ref[at * width : (at + 1) * width, :] = block
        if chain is not None:
            chain.serve_turn(served)

    sum_over_col(total_ref, summed_ref, *sums, between=own_rows)
    lower_ref[...] = get_half(summed_ref, 0)

    def beside(b):
        if chain is not None:

            @pl.when(b % 2 == 1)
            def _():
                chain.serve_turn(served + 1 + b // 2)

    eliminate(lower_ref, True, beside)
    top_ref[...] = transposed_dot(get_half(summed_ref, 1), lower_ref[...]) - eye(width)
    if chain is not None:

        @pl.loop(served + 1 + width // LEAF // 2, chain.turns())
        def _(turn):
            chain.serve_turn(turn)

        chain.end()


def prepare(strip, raw_rows, first, later, matrix, chain_root, collective_id):
    width, cyc_cols, _ = strip.shape
    cyc_rows = raw_rows.shape[0]
    f32, vmem = jnp.float32, pl.BlockSpec(memory_space=pltpu.VMEM)
    square = jax.ShapeDtypeStruct((width, width), f32)
    args = [strip, raw_rows]
    out_shape = [
        jax.ShapeDtypeStruct((cyc_cols * width, width), f32),
        jax.ShapeDtypeStruct((cyc_rows * width, width), f32),
        square,
        square,
    ]
    if later is not None:
        args += later
        out_shape += [
            jax.ShapeDtypeStruct((cyc_cols * width, 2 * width), f32),
            jax.ShapeDtypeStruct((cyc_rows * width, 2 * width), f32),
        ]
    specs = [vmem] * len(args)
    sums = sum_scratch(width)
    scratch = [sums[0], sums[0], pltpu.VMEM((width, width), f32)] + sums[1:]
    if chain_root is not None:
        args.append(matrix)
        specs.append(pl.BlockSpec(memory_space=pl.ANY))
        out_shape.append(jax.ShapeDtypeStruct((cyc_rows, width, width), f32))
        scratch += chain_sems(cyc_rows)
    return pl.pallas_call(
        functools.partial(prepare_kernel, first, later is not None, chain_root),
        out_shape=out_shape,
        in_specs=specs,
        out_specs=[vmem] * len(out_shape),
        scratch_shapes=scratch,
        compiler_params=remote_params(collective_id),
    )(*args)


def panel_kernel(first, group, mirrors, later, root_strip, *refs):
    refs = list(refs)
    take = lambda n: [refs.pop(0) for _ in range(n)]
    a_ref, cols_ref, lower_ref, top_ref, own_ref = take(5)
    if later:
        old_cols_ref, old_rows_ref = take(2)
    if root_strip is not None:
        (strip_ref,) = take(1)
    w_ref, inverse_ref, rows_ref, spread_ref, w_rows_ref, both_ref = take(6)
    if root_strip is not None:
        (strip_out,) = take(1)
    held, weights, part, arrived, sems = take(5)
    sum_send, sum_recv, on_send, on_recv, tree_send, tree_recv, local_sem = take(7)
    total_ref, *sums = take(6)
    if later:
        small_ref, old_weights = take(2)
    rows, cols = lax.axis_size("row"), lax.axis_size("col")
    row, col = lax.axis_index("row"), lax.axis_index("col")
    cyc_cols, width = a_ref.shape[1:]
    pieces, tile = part.shape[1:3]
    tiles = cols * pieces
    greet("row", "col")

    def owner(index):
        return (col + 1 + index // pieces) % cols

    def fetch(index, slot):
        start = (owner(index) * pieces + index % pieces) * tile
        return [
            pltpu.make_async_copy(
                a_ref.at[pl.ds(pl.multiple_of(start, tile), tile), c, :],
                held.at[slot, c],
                sems.at[slot, c],
            )
            for c in range(cyc_cols)
        ]

    for copy in fetch(0, 0):
        copy.start()
    strip = None
    if root_strip is not None:
        root, layer = root_strip
        strip = Strip(root, strip_ref.at[layer], strip_out, *refs)
        strip.begin()

    square_row = lax.broadcasted_iota(jnp.int32, (width, width), 0)
    square_lane = lax.broadcasted_iota(jnp.int32, (width, width), 1)
    identity = (square_row == square_lane).astype(jnp.float32)
    if later:
        small_ref[...] = jnp.zeros_like(small_ref)

    tall = min(4, cyc_cols)

    @pl.loop(0, cyc_cols // tall)
    def _(chunk):
        where = pl.ds(pl.multiple_of(chunk * tall * width, tall * width), tall * width)
        w = transposed_dot(cols_ref[where, :], lower_ref[...])
        units = [
            identity * flag((chunk * tall + c) * cols + col == first) for c in range(tall)
        ]
        w = w - jnp.concatenate(units, axis=0)
        w_ref[where, :] = w
        both = side_by_side(w)
        weights[where, :] = both
        if later:
            small_ref[...] += three_term(split(old_cols_ref[where, :]), both, transposed_left)

    if later:
        high, low = split(small_ref[...])
        old_weights[:, :width] = high
        old_weights[:, width:] = low

    def to_owner(index):
        q, piece = owner(index), index % pieces
        return remote(
            part.at[q, piece],
            arrived.at[index // pieces, piece],
            sum_send.at[index],
            sum_recv.at[index],
            col=q,
        )

    @pl.loop(0, tiles)
    def _(index):
        slot = lax.rem(index, 2)

        @pl.when(index + 1 < tiles)
        def _():
            for copy in fetch(index + 1, 1 - slot):
                copy.start()

        for copy in fetch(index, slot):
            copy.wait()
        total = None
        for chunk in range(cyc_cols // group):
            parts = [split(held[slot, chunk * group + g]) for g in range(group)]
            left = tuple(jnp.concatenate([p[i] for p in parts], axis=1) for i in range(2))
            right = weights[chunk * group * width : (chunk + 1) * group * width, :]
            term = three_term(left, right, dot_f32)
            total = term if total is None else total + term
        q, piece = owner(index), index % pieces
        if later:
            start = pl.multiple_of((q * pieces + piece) * tile, tile)
            old = split(old_rows_ref[pl.ds(start, tile), :])
            total = total - three_term(old, old_weights[...], dot_f32)
        part[q, piece] = total

        @pl.when(index < tiles - pieces)
        def _():
            to_owner(index).start()

        if strip is not None:
            strip.serve_turn(index)

    if strip is not None:

        @pl.loop(tiles, max(tiles, strip.turns()))
        def _(turn):
            strip.serve_turn(turn)

    inverse_ref[...] = -top_ref[...]
    eliminate(inverse_ref, False)
    for chunk in range(own_ref.shape[0] // (4 * width)):
        where = slice(chunk * 4 * width, (chunk + 1) * 4 * width)
        w = transposed_dot(own_ref[where, :], lower_ref[...])
        units = [identity * flag((chunk * 4 + i) * rows + row == first) for i in range(4)]
        w_rows_ref[where, :] = w - jnp.concatenate(units, axis=0)

    bits = rows.bit_length() - 1
    order = list(range(1, bits)) + [0]
    across = [row + (1 - 2 * ((row // 2**b) % 2)) * 2**b for b in order]

    def spot(mirror, q, piece):
        start = (q * pieces + piece) * tile
        if tile >= width:
            blocks = tile // width
            return spread_ref.at[pl.ds((q * pieces + piece) * blocks, blocks), mirror]
        inside = pl.ds(pl.multiple_of(start % width, tile), tile)
        return spread_ref.at[start // width, mirror, inside]

    def source(q, piece):
        view = rows_ref.at[q, piece]
        return view.reshape(tile // width, width, width) if tile >= width else view

    def onward(q, piece, side):
        return remote(
            rows_ref.at[q, piece],
            rows_ref.at[q, piece],
            on_send.at[side, q, piece],
            on_recv.at[q, piece],
            col=(col + 1 - 2 * side + cols) % cols,
        )

    def branch(mirror, q, piece, t, view):
        return remote(
            view,
            spot(mirror, q, piece),
            tree_send.at[mirror, q, piece, t],
            tree_recv.at[mirror, q, piece],
            row=across[t],
        )

    def own_copy(mirror, q, piece):
        return pltpu.make_async_copy(
            source(q, piece), spot(mirror, q, piece), local_sem.at[mirror, q, piece]
        )

    below = []
    for mirror in range(mirrors):
        root = col + mirror * cols
        differ = [((row // 2**b) % 2 + (root // 2**b) % 2) % 2 for b in order]
        below.append([sum(differ[t:]) for t in range(bits)])

    def root_start(q, piece):
        for mirror in range(mirrors):

            @pl.when(below[mirror][0] == 0)
            def _():
                own_copy(mirror, q, piece).start()
                for t in range(bits):
                    branch(mirror, q, piece, t, source(q, piece)).start()

    def relay(mirror, q, piece):
        for t in range(bits):
            copy = branch(mirror, q, piece, t, spot(mirror, q, piece))
            if t == 0:
                copy.wait_recv()

            @pl.when(below[mirror][t] == 0)
            def _():
                copy.start()

    @pl.loop(0, pieces)
    def _(piece):
        value = part[col, piece]
        for step in range(cols - 1):
            to_owner(step * pieces + piece).wait_recv()
            value = value + arrived[step, piece]
        rows_ref[col, piece] = value
        for side in range(2):

            @pl.when((col < cols - 1) if side == 0 else (col > 0))
            def _():
                onward(col, piece, side).start()

    both_sides = jnp.minimum(col, cols - 1 - col)
    longer = jnp.where(2 * col < cols - 1, 1, -1)

    def visit(number):
        group, piece = number // pieces, number % pieces
        paired = group <= 2 * both_sides
        far = jnp.where(paired, (group + 1) // 2, group - both_sides)
        way = jnp.where(paired, 1 - 2 * (group % 2), longer)
        return col + far * way, piece, way

    visits = cols * pieces
    lags = [LAG * below[mirror][0] for mirror in range(mirrors)]

    @pl.loop(0, visits + LAG * bits)
    def _(number):
        q, piece, way = visit(number)

        @pl.when(number < visits)
        def _():
            for side in range(2):

                @pl.when((number >= pieces) & (way == 1 - 2 * (1 - side)))
                def _():
                    copy = onward(q, piece, side)
                    copy.wait_recv()

                    @pl.when((col < cols - 1) if side == 0 else (col > 0))
                    def _():
                        copy.start()

            root_start(q, piece)

        for mirror in range(mirrors):
            late = number - lags[mirror]

            @pl.when((below[mirror][0] != 0) & (late >= 0) & (late < visits))
            def _():
                q, piece, _way = visit(late)
                relay(mirror, q, piece)

    @pl.loop(0, cols)
    def _(q):
        @pl.loop(0, pieces)
        def _(piece):
            @pl.when((q <= col) & (col < cols - 1))
            def _():
                onward(q, piece, 0).wait_send()

            @pl.when((q >= col) & (col > 0))
            def _():
                onward(q, piece, 1).wait_send()

            for mirror in range(mirrors):

                @pl.when(below[mirror][0] == 0)
                def _():
                    own_copy(mirror, q, piece).wait()

                for t in range(bits):

                    @pl.when(below[mirror][t] == 0)
                    def _():
                        branch(mirror, q, piece, t, spot(mirror, q, piece)).wait_send()

    @pl.loop(0, tiles - pieces)
    def _(index):
        to_owner(index).wait_send()

    small = jnp.zeros((width, width), jnp.float32)
    for chunk in range(cyc_cols // tall):
        where = slice(chunk * tall * width, (chunk + 1) * tall * width)
        y = spread_ref[chunk * tall // mirrors : (chunk + 1) * tall // mirrors]
        y = y.reshape(tall * width, width)
        small = small + three_term(split(y), weights[where, :], transposed_left)
    put_half(total_ref, 0, small.T)
    c = first // cols
    y = spread_ref[c // mirrors, c % mirrors]
    put_half(total_ref, 1, jnp.where(col == first % cols, y, 0.0))
    sum_over_col(total_ref, both_ref, *sums)

    if strip is not None:
        strip.end()


def panel_product(matrix, cols, lower, w_top, own, first, old, root_strip, collective_id):
    rows_size, cols_size = lax.axis_size("row"), lax.axis_size("col")
    mirrors = rows_size // cols_size
    bits = rows_size.bit_length() - 1
    cyc_rows, width, cyc_cols, _ = matrix.shape
    n_rows = cyc_rows * width
    depth = n_rows // cols_size
    tile = min(256, depth)
    pieces = depth // tile
    flat = matrix.reshape(n_rows, cyc_cols, width)
    vmem, anywhere = pl.BlockSpec(memory_space=pltpu.VMEM), pl.BlockSpec(memory_space=pl.ANY)
    f32, dma = jnp.float32, pltpu.SemaphoreType.DMA
    args, specs = [flat, cols, lower, w_top, own], [anywhere, vmem, vmem, vmem, vmem]
    if old is not None:
        args += list(old)
        specs += [vmem, vmem]
    out_shape = [
        jax.ShapeDtypeStruct(cols.shape, f32),
        jax.ShapeDtypeStruct((width, width), f32),
        jax.ShapeDtypeStruct((cols_size, pieces, tile, width), f32),
        jax.ShapeDtypeStruct((cyc_rows, mirrors, width, width), f32),
        jax.ShapeDtypeStruct((n_rows, width), f32),
        jax.ShapeDtypeStruct((rows_size, 2 * width // rows_size, width), f32),
    ]
    scratch = [
        pltpu.VMEM((2, cyc_cols, tile, width), f32),
        pltpu.VMEM((cols.shape[0], 2 * width), jnp.bfloat16),
        pltpu.VMEM((cols_size, pieces, tile, width), f32),
        pltpu.VMEM((cols_size - 1, pieces, tile, width), f32),
        dma((2, cyc_cols)),
        dma((cols_size * pieces,)),
        dma((cols_size * pieces,)),
        dma((2, cols_size, pieces)),
        dma((cols_size, pieces)),
        dma((mirrors, cols_size, pieces, bits)),
        dma((mirrors, cols_size, pieces)),
        dma((mirrors, cols_size, pieces)),
    ] + sum_scratch(width)
    if old is not None:
        scratch += [
            pltpu.VMEM((2 * width, width), f32),
            pltpu.VMEM((2 * width, 2 * width), jnp.bfloat16),
        ]
    if root_strip is not None:
        args.append(matrix)
        specs.append(anywhere)
        out_shape.append(jax.ShapeDtypeStruct(matrix.shape[1:], f32))
        scratch += STRIP_SEMS
    return pl.pallas_call(
        functools.partial(
            panel_kernel, first, min(8, cyc_cols), mirrors, old is not None, root_strip
        ),
        out_shape=out_shape,
        in_specs=specs,
        out_specs=[vmem] * len(out_shape),
        scratch_shapes=scratch,
        compiler_params=remote_params(collective_id),
    )(*args)


def update_kernel(
    group,
    a_ref,
    both_ref,
    inverse_ref,
    y_cols_ref,
    w_cols_ref,
    old_cols_ref,
    y_rows_ref,
    w_rows_ref,
    old_rows_ref,
    out_ref,
    held,
    done,
    vh_ref,
    vl_ref,
    finish_ref,
    sems,
    out_sems,
):
    tile = w_rows_ref.shape[0]
    cyc_cols, width = a_ref.shape[1:]
    step, steps = pl.program_id(0), pl.num_programs(0)
    slot, copies = fetch_tiles(a_ref, held, sems, tile)

    @pl.when(step == 0)
    def _():
        inverse = inverse_ref[...]
        core = 0.5 * transposed_dot(dot_highest(inverse, get_half(both_ref, 0)), inverse)
        finish_ref[...] = side_by_side(jnp.concatenate([inverse.T, -core], axis=0))
        rows = min(4, cyc_cols) * width

        @pl.loop(0, cyc_cols * width // rows)
        def _(chunk):
            where = pl.ds(pl.multiple_of(chunk * rows, rows), rows)
            w = w_cols_ref[where, :]
            z = three_term(
                split(jnp.concatenate([y_cols_ref[where, :], w], axis=1)), finish_ref[...], dot_f32
            )
            for at, value in ((0, old_cols_ref[where, :]), (2 * width, w), (3 * width, z)):
                v_high, v_low = split(value.T)
                vh_ref[at : at + value.shape[1], where] = v_high
                vl_ref[at : at + value.shape[1], where] = v_low

    w = w_rows_ref[...]
    z = three_term(
        split(jnp.concatenate([y_rows_ref[...], w], axis=1)), finish_ref[...], dot_f32
    )
    high, low = split(jnp.concatenate([old_rows_ref[...], z, w], axis=1))

    def stores(index, where):
        return [
            pltpu.make_async_copy(
                done.at[where, c],
                out_ref.at[pl.ds(index * tile, tile), c, :],
                out_sems.at[where, c],
            )
            for c in range(cyc_cols)
        ]

    @pl.when(step >= 2)
    def _():
        for copy in stores(step - 2, slot):
            copy.wait()

    for copy in copies:
        copy.wait()
    started = stores(step, slot)
    for chunk in range(cyc_cols // group):
        columns = slice(chunk * group * width, (chunk + 1) * group * width)
        v_high, v_low = vh_ref[:, columns], vl_ref[:, columns]
        delta = dot_f32(high, v_low) + dot_f32(low, v_high) + dot_f32(high, v_high)
        for g in range(group):
            c = chunk * group + g
            done[slot, c] = held[slot, c] - delta[:, g * width : (g + 1) * width]
            started[c].start()

    @pl.when(step == steps - 1)
    def _():
        for copy in stores(step, slot):
            copy.wait()

        @pl.when(steps > 1)
        def _():
            for copy in stores(step - 1, 1 - slot):
                copy.wait()


def apply_update(matrix, both, inverse, y_cols, w_cols, old_cols, y_rows, w_rows, old_rows):
    cyc_rows, width, cyc_cols, _ = matrix.shape
    n_rows = cyc_rows * width
    tile = min(256, n_rows)

    def whole(x):
        return pl.BlockSpec(x.shape, lambda i: (0,) * x.ndim, pipeline_mode=pl.Buffered(1))

    def some(x):
        return pl.BlockSpec((tile, x.shape[1]), lambda i: (i, 0))

    held = pltpu.VMEM((2, cyc_cols, tile, width), jnp.float32)
    right = pltpu.VMEM((4 * width, cyc_cols * width), jnp.bfloat16)
    sems = pltpu.SemaphoreType.DMA((2, cyc_cols))
    fixed, moving = [both, inverse, y_cols, w_cols, old_cols], [y_rows, w_rows, old_rows]
    return pl.pallas_call(
        functools.partial(update_kernel, min(4, cyc_cols)),
        grid=(n_rows // tile,),
        out_shape=jax.ShapeDtypeStruct((n_rows, cyc_cols, width), jnp.float32),
        in_specs=[pl.BlockSpec(memory_space=pl.ANY)]
        + [whole(x) for x in fixed]
        + [some(x) for x in moving],
        out_specs=pl.BlockSpec(memory_space=pl.ANY),
        scratch_shapes=[
            held,
            held,
            right,
            right,
            pltpu.VMEM((2 * width, 2 * width), jnp.bfloat16),
            sems,
            sems,
        ],
        compiler_params=pltpu.CompilerParams(vmem_limit_bytes=VMEM_LIMIT),
    )(matrix.reshape(n_rows, cyc_cols, width), *fixed, *moving)


def local(matrix):
    row_count = lax.axis_size("row")
    col_count = lax.axis_size("col")
    cyc_rows, width, cyc_cols, _ = matrix.shape
    n_rows, n_cols = cyc_rows * width, cyc_cols * width

    strip, raw = spread(matrix, 0, 0, 0, 0, 0)
    cols, own, lower, w_top, raw = prepare(
        strip, raw, 1, None, matrix, (1 % col_count, 1 // col_count), 1
    )
    strip_of = (1 % row_count, 1 // row_count)
    wc, inverse, y_rows, y_cols, wr, both, strip = panel_product(
        matrix, cols, lower, w_top, own, 1, None, strip_of, 2
    )
    later = [
        both,
        inverse,
        w_top,
        y_cols.reshape(n_cols, width),
        wc,
        y_rows.reshape(n_rows, width),
        wr,
    ]
    cols, own, lower, w_top, old_cols, old_rows = prepare(strip, raw, 2, later, matrix, None, 3)
    wc, inverse, y_rows, y_cols, wr_last, both = panel_product(
        matrix, cols, lower, w_top, own, 2, (old_cols, old_rows), None, 4
    )
    y_rows, y_cols = y_rows.reshape(n_rows, width), y_cols.reshape(n_cols, width)
    reduced = apply_update(
        matrix, both, inverse, y_cols, wc, old_cols, y_rows, wr_last, old_rows
    ).reshape(matrix.shape)
    bases = jnp.concatenate([wr, wr_last], axis=1).reshape(cyc_rows, width, PANELS * width)
    return (reduced, bases)


def solution(mesh):
    return jax.shard_map(
        local,
        mesh=mesh,
        in_specs=(P(None, "row", None, "col"),),
        out_specs=(P(None, "row", None, "col"), P(None, "row", None)),
        check_vma=False,
    )
```

```python
import functools

import jax
import jax.numpy as jnp
from jax import lax
from jax.experimental import pallas as pl
from jax.experimental.pallas import tpu as pltpu
from jax.sharding import PartitionSpec as P

PANELS = 2
MESH = pl.DeviceIdType.MESH
VMEM_LIMIT = 60 * 1024 * 1024


def dot_highest(left, right):
    return jnp.dot(left, right, precision=lax.Precision.HIGHEST, preferred_element_type=jnp.float32)


def greet(*axes):
    barrier = pltpu.get_barrier_semaphore()
    total = 0
    for axis in axes:
        me, size = lax.axis_index(axis), lax.axis_size(axis)
        for step in range(1, size):
            pl.semaphore_signal(
                barrier, inc=1, device_id={axis: lax.rem(me + step, size)}, device_id_type=MESH
            )
        total += size - 1
    pl.semaphore_wait(barrier, total)


def remote(src, dst, send_sem, recv_sem, **device):
    return pltpu.make_async_remote_copy(
        src_ref=src,
        dst_ref=dst,
        send_sem=send_sem,
        recv_sem=recv_sem,
        device_id=device,
        device_id_type=MESH,
    )


def remote_params(collective_id):
    return pltpu.CompilerParams(
        collective_id=collective_id, has_side_effects=True, vmem_limit_bytes=VMEM_LIMIT
    )

STREAM_CHUNKS = 8

LAG = 2


def ring_place(pair, pairs):
    return pair + (pair // 2) * (1 - 2 * (pair % 2)) if pairs == 4 else pair


class Strip:
    def __init__(self, root, strip_ref, out_ref, ring_send, pair_send, recv, local_sem):
        size = lax.axis_size("row")
        me = lax.axis_index("row")
        pairs = size // 2
        pair, core = me // 2, me % 2
        place = ring_place(pair, pairs)
        distance = (place - ring_place(root // 2, pairs) + pairs) % pairs
        stream = (core + root % 2) % 2
        hop = (distance * (1 - 2 * stream) + stream * pairs) % pairs
        self.target = 2 * ring_place((place + 1 - 2 * stream + pairs) % pairs, pairs) + core
        self.sibling = 2 * pair + 1 - core
        self.root, self.me, self.pairs = root, me, pairs
        self.stream, self.hop, self.distance = stream, hop, distance
        self.strip_ref, self.out_ref = strip_ref, out_ref
        self.ring_send, self.pair_send = ring_send, pair_send
        self.recv, self.local_sem = recv, local_sem
        self.piece = out_ref.shape[0] // (2 * STREAM_CHUNKS)

    def rows_of(self, which, i):
        start = (which * STREAM_CHUNKS + i) * self.piece
        return pl.ds(pl.multiple_of(start, self.piece), self.piece)

    def to_ring(self, i, source, which):
        rows = self.rows_of(which, i)
        return remote(
            source.at[rows],
            self.out_ref.at[rows],
            self.ring_send.at[i],
            self.recv.at[which, i],
            row=self.target,
        )

    def to_sibling(self, i, source, which, slot):
        rows = self.rows_of(which, i)
        return remote(
            source.at[rows],
            self.out_ref.at[rows],
            self.pair_send.at[slot, i],
            self.recv.at[which, i],
            row=self.sibling,
        )

    def root_copies(self):
        copies = []
        for i in range(STREAM_CHUNKS):
            copies.append(self.to_ring(i, self.strip_ref, 0))
            copies.append(self.to_sibling(i, self.strip_ref, 1, 1))
        for i in range(STREAM_CHUNKS):
            copies.append(self.to_sibling(i, self.strip_ref, 0, 0))
        return copies

    def begin(self):
        @pl.when(self.me == self.root)
        def _():
            for copy in self.root_copies():
                copy.start()
            pltpu.make_async_copy(self.strip_ref, self.out_ref, self.local_sem).start()

    def serve(self, i):
        onward = self.to_ring(i, self.out_ref, self.stream)
        onward.wait_recv()

        @pl.when(self.hop < self.pairs - 1)
        def _():
            onward.start()

        @pl.when(self.distance > 0)
        def _():
            self.to_sibling(i, self.out_ref, self.stream, 0).start()

    def serve_turn(self, turn):
        first = 2 * (turn - 2 * self.hop)
        for half in range(2):
            i = first + half

            @pl.when((self.me != self.root) & (i >= 0) & (i < STREAM_CHUNKS))
            def _():
                self.serve(i)

    def turns(self):
        return STREAM_CHUNKS // 2 + 2 * (self.pairs - 1)

    def end(self):
        @pl.when(self.me == self.root)
        def _():
            for copy in self.root_copies():
                copy.wait_send()
            pltpu.make_async_copy(self.strip_ref, self.out_ref, self.local_sem).wait()

        @pl.when(self.me != self.root)
        def _():
            for i in range(STREAM_CHUNKS):
                self.to_ring(i, self.out_ref, 1 - self.stream).wait_recv()

                @pl.when(self.hop < self.pairs - 1)
                def _():
                    self.to_ring(i, self.out_ref, self.stream).wait_send()

                @pl.when(self.distance > 0)
                def _():
                    self.to_sibling(i, self.out_ref, self.stream, 0).wait_send()


STRIP_SEMS = [
    pltpu.SemaphoreType.DMA((STREAM_CHUNKS,)),
    pltpu.SemaphoreType.DMA((2, STREAM_CHUNKS)),
    pltpu.SemaphoreType.DMA((2, STREAM_CHUNKS)),
    pltpu.SemaphoreType.DMA,
]


class Chain:
    def __init__(self, root, layer, a_ref, out_ref, send, recv, local_sems):
        self.col, self.cols = lax.axis_index("col"), lax.axis_size("col")
        self.root, self.layer, self.a_ref, self.out_ref = root, layer, a_ref, out_ref
        self.send, self.recv, self.local_sems = send, recv, local_sems
        self.count = recv.shape[0]
        self.piece = out_ref.shape[0] // self.count
        self.ways = [(self.col >= root) & (self.col < self.cols - 1), (self.col <= root) & (self.col > 0)]

    def part(self, i):
        return pl.ds(pl.multiple_of(i * self.piece, self.piece), self.piece)

    def local(self, i):
        return pltpu.make_async_copy(
            self.a_ref.at[self.part(i), :, self.layer, :],
            self.out_ref.at[self.part(i)],
            self.local_sems.at[i],
        )

    def onward(self, i, side):
        view = self.out_ref.at[self.part(i)]
        target = (self.col + 1 - 2 * side + self.cols) % self.cols
        return remote(view, view, self.send.at[side, i], self.recv.at[i], col=target)

    def begin(self):
        @pl.when(self.col == self.root)
        def _():
            for i in range(self.count):
                self.local(i).start()

    def serve(self, i):
        @pl.when(self.col == self.root)
        def _():
            self.local(i).wait()

        @pl.when(self.col != self.root)
        def _():
            self.onward(i, 0).wait_recv()

        for side in range(2):

            @pl.when(self.ways[side])
            def _():
                self.onward(i, side).start()

    def serve_turn(self, turn):
        far = jnp.maximum(self.col - self.root, self.root - self.col)
        i = turn - far

        @pl.when((i >= 0) & (i < self.count))
        def _():
            self.serve(i)

    def turns(self):
        return self.count + self.cols

    def end(self):
        for i in range(self.count):
            for side in range(2):

                @pl.when(self.ways[side])
                def _():
                    self.onward(i, side).wait_send()


def chain_sems(cyc_rows):
    count = min(8, cyc_rows)
    dma = pltpu.SemaphoreType.DMA
    return [dma((2, count)), dma((count,)), dma((count,))]


def spread_kernel(root, layer, col_root, col_layer, a_ref, strip_ref, rows_ref, *sems):
    greet("row", "col")
    strip = Strip(root, a_ref.at[layer], strip_ref, *sems[: len(STRIP_SEMS)])
    chain = Chain(col_root, col_layer, a_ref, rows_ref, *sems[len(STRIP_SEMS) :])
    strip.begin()
    chain.begin()

    @pl.loop(0, max(strip.turns(), chain.turns()))
    def _(turn):
        chain.serve_turn(turn)
        strip.serve_turn(turn)

    strip.end()
    chain.end()


def spread(matrix, root, layer, col_root, col_layer, collective_id):
    cyc_rows, width, _, _ = matrix.shape
    return pl.pallas_call(
        functools.partial(spread_kernel, root, layer, col_root, col_layer),
        out_shape=[
            jax.ShapeDtypeStruct(matrix.shape[1:], matrix.dtype),
            jax.ShapeDtypeStruct((cyc_rows, width, width), matrix.dtype),
        ],
        in_specs=[pl.BlockSpec(memory_space=pl.ANY)],
        out_specs=[pl.BlockSpec(memory_space=pltpu.VMEM)] * 2,
        scratch_shapes=STRIP_SEMS + chain_sems(cyc_rows),
        compiler_params=remote_params(collective_id),
    )(matrix)


def sum_over_col(x_ref, out_ref, held, col_send, col_recv, row_send, row_recv, between=None):
    rows, cols = lax.axis_size("row"), lax.axis_size("col")
    row, col = lax.axis_index("row"), lax.axis_index("col")
    copies = []
    for step in range(1, cols):
        copy = remote(
            x_ref.at[row],
            held.at[col],
            col_send.at[step],
            col_recv.at[step],
            col=lax.rem(col + step, cols),
        )
        copy.start()
        copies.append(copy)
    held[col] = x_ref[row]
    for copy in copies:
        copy.wait()
    value = held[0]
    for q in range(1, cols):
        value = value + held[q]
    out_ref[row] = value
    copies = []
    for step in range(1, rows):
        copy = remote(
            out_ref.at[row],
            out_ref.at[row],
            row_send.at[step],
            row_recv.at[step],
            row=lax.rem(row + step, rows),
        )
        copy.start()
        copies.append(copy)
    if between is not None:
        between()
    for copy in copies:
        copy.wait()


def sum_scratch(width):
    rows, cols = lax.axis_size("row"), lax.axis_size("col")
    piece = 2 * width // rows
    dma = pltpu.SemaphoreType.DMA
    return [
        pltpu.VMEM((rows, piece, width), jnp.float32),
        pltpu.VMEM((cols, piece, width), jnp.float32),
        dma((cols,)),
        dma((cols,)),
        dma((rows,)),
        dma((rows,)),
    ]


def put_half(x_ref, half, value):
    rows, piece, width = x_ref.shape
    for r in range(rows // 2):
        x_ref[half * (rows // 2) + r] = value[r * piece : (r + 1) * piece]


def get_half(x_ref, half):
    rows, piece, width = x_ref.shape
    return x_ref[pl.ds(half * (rows // 2), rows // 2)].reshape(width, width)


LEAF = 16


def eliminate(ref, symmetric, beside=None):
    size = ref.shape[0]
    strip_row = lax.broadcasted_iota(jnp.int32, (LEAF, size), 0)
    strip_lane = lax.broadcasted_iota(jnp.int32, (LEAF, size), 1)
    row = lax.broadcasted_iota(jnp.int32, (size, size), 0)
    lane = lax.broadcasted_iota(jnp.int32, (size, size), 1)

    def block(b, carry):
        start = pl.multiple_of(b * LEAF, LEAF)
        whole = ref[...]
        strip = ref[pl.ds(start, LEAF), :]
        columns = [jnp.broadcast_to(strip[:, i : i + 1], (LEAF, size)) for i in range(LEAF)]
        panel = jnp.where(strip_lane < LEAF, (strip_row == strip_lane).astype(jnp.float32), strip)
        for i in range(LEAF):
            column = columns[i]
            pivot = jnp.broadcast_to(column[i : i + 1, :], (LEAF, size))
            if symmetric:
                scale = lax.rsqrt(pivot)
                scale = scale * (1.5 - 0.5 * pivot * scale * scale)
                column = column * scale
                touched = strip_row > i
            else:
                scale = 1.0 / pivot
                touched = strip_row != i

            def step(x):
                lead = jnp.broadcast_to(x[i : i + 1, :], (LEAF, size)) * scale
                return jnp.where(touched, x - column * lead, jnp.where(strip_row == i, lead, x))

            panel = step(panel)
            for j in range(i + 1, LEAF):
                columns[j] = step(columns[j])
        base = jnp.where(lane < LEAF, 0.0, whole)
        if symmetric:
            factor = jnp.where((strip_lane >= LEAF) & (strip_lane < size - start), panel, 0.0)
            factor = pltpu.roll(factor, start, axis=1)
            change = lax.dot_general(
                factor,
                panel,
                (((0,), (0,)), ((), ())),
                precision=lax.Precision.HIGHEST,
                preferred_element_type=jnp.float32,
            )
            ref[...] = jnp.where(row < start, whole, base - change)
        else:
            inside = (row >= start) & (row < start + LEAF)
            factor = jnp.where(inside | (lane >= LEAF), 0.0, whole)
            padded = jnp.concatenate([panel, jnp.zeros((size - LEAF, size), jnp.float32)], axis=0)
            ref[...] = base - dot_highest(factor, padded)
        ref[pl.ds(start, LEAF), :] = panel
        ref[...] = pltpu.roll(ref[...], size - LEAF, axis=1)
        if beside is not None:
            beside(b)
        return carry

    lax.fori_loop(0, size // LEAF, block, 0)
    if symmetric:
        ref[...] = jnp.where(row >= lane, ref[...], 0.0)


def transposed_dot(left, right):
    return lax.dot_general(
        left,
        right,
        (((1,), (1,)), ((), ())),
        precision=lax.Precision.HIGHEST,
        preferred_element_type=jnp.float32,
    )


def split(value):
    high = value.astype(jnp.bfloat16)
    return high, (value - high.astype(jnp.float32)).astype(jnp.bfloat16)


def dot_f32(left, right):
    return jnp.dot(left, right, preferred_element_type=jnp.float32)


def tile_copies(a_ref, held, sems, tile, index, slot):
    return [
        pltpu.make_async_copy(
            a_ref.at[pl.ds(index * tile, tile), c, :], held.at[slot, c], sems.at[slot, c]
        )
        for c in range(a_ref.shape[1])
    ]


def fetch_tiles(a_ref, held, sems, tile):
    step, steps = pl.program_id(0), pl.num_programs(0)
    slot = lax.rem(step, 2)

    @pl.when(step == 0)
    def _():
        for copy in tile_copies(a_ref, held, sems, tile, step, slot):
            copy.start()

    @pl.when(step + 1 < steps)
    def _():
        for copy in tile_copies(a_ref, held, sems, tile, step + 1, 1 - slot):
            copy.start()

    return slot, tile_copies(a_ref, held, sems, tile, step, slot)


def transposed_left(left, right):
    return lax.dot_general(
        left, right, (((0,), (0,)), ((), ())), preferred_element_type=jnp.float32
    )


def three_term(left, right, dot):
    high, low = left
    width = right.shape[1] // 2
    wide = dot(high, right)
    return wide[:, width:] + dot(low, right[:, :width]) + wide[:, :width]


def eye(width):
    row = lax.broadcasted_iota(jnp.int32, (width, width), 0)
    lane = lax.broadcasted_iota(jnp.int32, (width, width), 1)
    return (row == lane).astype(jnp.float32)


def flag(condition):
    return condition.astype(jnp.float32)


def side_by_side(value):
    return jnp.concatenate(split(value), axis=1)


def prepare_kernel(first, later, chain_root, *refs):
    refs = list(refs)
    take = lambda n: [refs.pop(0) for _ in range(n)]
    strip_ref, raw_rows_ref = take(2)
    if later:
        both_ref, inverse_ref, old_top_ref, y_cols_ref, w_cols_ref, y_rows_ref, w_rows_ref = take(7)
    if chain_root is not None:
        (a_ref,) = take(1)
    cols_ref, rows_ref, lower_ref, top_ref = take(4)
    if later:
        old_cols_ref, old_rows_ref = take(2)
    if chain_root is not None:
        (chain_ref,) = take(1)
    total_ref, summed_ref, gram_ref = take(3)
    sums = take(5)
    rows, cols = lax.axis_size("row"), lax.axis_size("col")
    row, col = lax.axis_index("row"), lax.axis_index("col")
    width = lower_ref.shape[0]
    cyc_cols, cyc_rows = strip_ref.shape[1], raw_rows_ref.shape[0]
    greet("row", "col")
    chain = None
    if chain_root is not None:
        chain = Chain(*chain_root, a_ref, chain_ref, *refs)
        chain.begin()

    if later:
        inverse = inverse_ref[...]
        middle, y_next = get_half(both_ref, 0), get_half(both_ref, 1)
        core = 0.5 * transposed_dot(dot_highest(inverse, middle), inverse)
        z_next = transposed_dot(y_next, inverse) - dot_highest(old_top_ref[...], core)
        finish = side_by_side(jnp.concatenate([inverse.T, -core], axis=0))
        inner = side_by_side(jnp.concatenate([old_top_ref[...].T, z_next.T], axis=0))

    def old_pair(y, w):
        return three_term(split(jnp.concatenate([y, w], axis=1)), finish, dot_f32)

    def correction(z, w):
        return three_term(split(jnp.concatenate([z, w], axis=1)), inner, dot_f32)

    gram_ref[...] = jnp.zeros_like(gram_ref)
    step = min(4, cyc_cols)
    for group in range(cyc_cols // step):
        where = slice(group * step * width, (group + 1) * step * width)
        held = range(group * step, (group + 1) * step)
        tall = jnp.concatenate([strip_ref[:, c, :].T for c in held], axis=0)
        if later:
            w = w_cols_ref[where, :]
            z = old_pair(y_cols_ref[where, :], w)
            old_cols_ref[where, :width] = w
            old_cols_ref[where, width:] = z
            tall = tall - correction(z, w)
        if group * step * cols < first:
            blocks = [
                jnp.where(c * cols + col >= first, tall[i * width : (i + 1) * width], 0.0)
                for i, c in enumerate(held)
            ]
            tall = jnp.concatenate(blocks, axis=0)
        cols_ref[where, :] = tall
        gram_ref[...] += lax.dot_general(
            tall,
            tall,
            (((0,), (0,)), ((), ())),
            precision=lax.Precision.HIGHEST,
            preferred_element_type=jnp.float32,
        )
        if chain is not None and group % 2 == 1:
            chain.serve_turn(group // 2)
    served = (cyc_cols // step) // 2
    put_half(total_ref, 0, gram_ref[...])
    top_at = (first // cols) * width
    holds = col == first % cols
    put_half(total_ref, 1, jnp.where(holds, cols_ref[top_at : top_at + width, :], 0.0))

    def own_rows():
        for group in range(cyc_rows // 4):
            where = slice(group * 4 * width, (group + 1) * 4 * width)
            tall = raw_rows_ref[group * 4 : (group + 1) * 4].reshape(4 * width, width)
            if later:
                w = w_rows_ref[where, :]
                z = old_pair(y_rows_ref[where, :], w)
                old_rows_ref[where, :width] = z
                old_rows_ref[where, width:] = w
                tall = tall - correction(z, w)
            for i in range(4):
                block = tall[i * width : (i + 1) * width]
                at = group * 4 + i
                if at * rows < first:
                    block = jnp.where(at * rows + row >= first, block, 0.0)
                rows_ref[at * width : (at + 1) * width, :] = block
        if chain is not None:
            chain.serve_turn(served)

    sum_over_col(total_ref, summed_ref, *sums, between=own_rows)
    lower_ref[...] = get_half(summed_ref, 0)

    def beside(b):
        if chain is not None:

            @pl.when(b % 2 == 1)
            def _():
                chain.serve_turn(served + 1 + b // 2)

    eliminate(lower_ref, True, beside)
    top_ref[...] = transposed_dot(get_half(summed_ref, 1), lower_ref[...]) - eye(width)
    if chain is not None:

        @pl.loop(served + 1 + width // LEAF // 2, chain.turns())
        def _(turn):
            chain.serve_turn(turn)

        chain.end()


def prepare(strip, raw_rows, first, later, matrix, chain_root, collective_id):
    width, cyc_cols, _ = strip.shape
    cyc_rows = raw_rows.shape[0]
    f32, vmem = jnp.float32, pl.BlockSpec(memory_space=pltpu.VMEM)
    square = jax.ShapeDtypeStruct((width, width), f32)
    args = [strip, raw_rows]
    out_shape = [
        jax.ShapeDtypeStruct((cyc_cols * width, width), f32),
        jax.ShapeDtypeStruct((cyc_rows * width, width), f32),
        square,
        square,
    ]
    if later is not None:
        args += later
        out_shape += [
            jax.ShapeDtypeStruct((cyc_cols * width, 2 * width), f32),
            jax.ShapeDtypeStruct((cyc_rows * width, 2 * width), f32),
        ]
    specs = [vmem] * len(args)
    sums = sum_scratch(width)
    scratch = [sums[0], sums[0], pltpu.VMEM((width, width), f32)] + sums[1:]
    if chain_root is not None:
        args.append(matrix)
        specs.append(pl.BlockSpec(memory_space=pl.ANY))
        out_shape.append(jax.ShapeDtypeStruct((cyc_rows, width, width), f32))
        scratch += chain_sems(cyc_rows)
    return pl.pallas_call(
        functools.partial(prepare_kernel, first, later is not None, chain_root),
        out_shape=out_shape,
        in_specs=specs,
        out_specs=[vmem] * len(out_shape),
        scratch_shapes=scratch,
        compiler_params=remote_params(collective_id),
    )(*args)


def panel_kernel(first, group, mirrors, later, root_strip, *refs):
    refs = list(refs)
    take = lambda n: [refs.pop(0) for _ in range(n)]
    a_ref, cols_ref, lower_ref, top_ref, own_ref = take(5)
    if later:
        old_cols_ref, old_rows_ref = take(2)
    if root_strip is not None:
        (strip_ref,) = take(1)
    w_ref, inverse_ref, rows_ref, spread_ref, w_rows_ref, both_ref = take(6)
    if root_strip is not None:
        (strip_out,) = take(1)
    held, weights, part, arrived, sems = take(5)
    sum_send, sum_recv, on_send, on_recv, tree_send, tree_recv, local_sem = take(7)
    total_ref, *sums = take(6)
    if later:
        small_ref, old_weights = take(2)
    rows, cols = lax.axis_size("row"), lax.axis_size("col")
    row, col = lax.axis_index("row"), lax.axis_index("col")
    cyc_cols, width = a_ref.shape[1:]
    pieces, tile = part.shape[1:3]
    tiles = cols * pieces
    greet("row", "col")

    def owner(index):
        return (col + 1 + index // pieces) % cols

    def fetch(index, slot):
        start = (owner(index) * pieces + index % pieces) * tile
        return [
            pltpu.make_async_copy(
                a_ref.at[pl.ds(pl.multiple_of(start, tile), tile), c, :],
                held.at[slot, c],
                sems.at[slot, c],
            )
            for c in range(cyc_cols)
        ]

    for ahead in range(2):
        for copy in fetch(ahead, ahead):
            copy.start()
    strip = None
    if root_strip is not None:
        root, layer = root_strip
        strip = Strip(root, strip_ref.at[layer], strip_out, *refs)
        strip.begin()

    square_row = lax.broadcasted_iota(jnp.int32, (width, width), 0)
    square_lane = lax.broadcasted_iota(jnp.int32, (width, width), 1)
    identity = (square_row == square_lane).astype(jnp.float32)
    if later:
        small_ref[...] = jnp.zeros_like(small_ref)

    tall = min(4, cyc_cols)

    @pl.loop(0, cyc_cols // tall)
    def _(chunk):
        where = pl.ds(pl.multiple_of(chunk * tall * width, tall * width), tall * width)
        w = transposed_dot(cols_ref[where, :], lower_ref[...])
        units = [
            identity * flag((chunk * tall + c) * cols + col == first) for c in range(tall)
        ]
        w = w - jnp.concatenate(units, axis=0)
        w_ref[where, :] = w
        both = side_by_side(w)
        weights[where, :] = both
        if later:
            small_ref[...] += three_term(split(old_cols_ref[where, :]), both, transposed_left)

    if later:
        high, low = split(small_ref[...])
        old_weights[:, :width] = high
        old_weights[:, width:] = low

    def to_owner(index):
        q, piece = owner(index), index % pieces
        return remote(
            part.at[q, piece],
            arrived.at[index // pieces, piece],
            sum_send.at[index],
            sum_recv.at[index],
            col=q,
        )

    @pl.loop(0, tiles)
    def _(index):
        slot = lax.rem(index, 2)
        for copy in fetch(index, slot):
            copy.wait()
        total = None
        for chunk in range(cyc_cols // group):
            parts = [split(held[slot, chunk * group + g]) for g in range(group)]
            left = tuple(jnp.concatenate([p[i] for p in parts], axis=1) for i in range(2))
            right = weights[chunk * group * width : (chunk + 1) * group * width, :]
            term = three_term(left, right, dot_f32)
            total = term if total is None else total + term
        q, piece = owner(index), index % pieces
        if later:
            start = pl.multiple_of((q * pieces + piece) * tile, tile)
            old = split(old_rows_ref[pl.ds(start, tile), :])
            total = total - three_term(old, old_weights[...], dot_f32)
        part[q, piece] = total

        @pl.when(index + 2 < tiles)
        def _():
            for copy in fetch(index + 2, slot):
                copy.start()

        @pl.when(index < tiles - pieces)
        def _():
            to_owner(index).start()

        if strip is not None:
            strip.serve_turn(index)

    if strip is not None:

        @pl.loop(tiles, max(tiles, strip.turns()))
        def _(turn):
            strip.serve_turn(turn)

    inverse_ref[...] = -top_ref[...]
    eliminate(inverse_ref, False)
    for chunk in range(own_ref.shape[0] // (4 * width)):
        where = slice(chunk * 4 * width, (chunk + 1) * 4 * width)
        w = transposed_dot(own_ref[where, :], lower_ref[...])
        units = [identity * flag((chunk * 4 + i) * rows + row == first) for i in range(4)]
        w_rows_ref[where, :] = w - jnp.concatenate(units, axis=0)

    bits = rows.bit_length() - 1
    order = list(range(1, bits)) + [0]
    across = [row + (1 - 2 * ((row // 2**b) % 2)) * 2**b for b in order]

    def spot(mirror, q, piece):
        start = (q * pieces + piece) * tile
        if tile >= width:
            blocks = tile // width
            return spread_ref.at[pl.ds((q * pieces + piece) * blocks, blocks), mirror]
        inside = pl.ds(pl.multiple_of(start % width, tile), tile)
        return spread_ref.at[start // width, mirror, inside]

    def source(q, piece):
        view = rows_ref.at[q, piece]
        return view.reshape(tile // width, width, width) if tile >= width else view

    def onward(q, piece, side):
        return remote(
            rows_ref.at[q, piece],
            rows_ref.at[q, piece],
            on_send.at[side, q, piece],
            on_recv.at[q, piece],
            col=(col + 1 - 2 * side + cols) % cols,
        )

    def branch(mirror, q, piece, t, view):
        return remote(
            view,
            spot(mirror, q, piece),
            tree_send.at[mirror, q, piece, t],
            tree_recv.at[mirror, q, piece],
            row=across[t],
        )

    def own_copy(mirror, q, piece):
        return pltpu.make_async_copy(
            source(q, piece), spot(mirror, q, piece), local_sem.at[mirror, q, piece]
        )

    below = []
    for mirror in range(mirrors):
        root = col + mirror * cols
        differ = [((row // 2**b) % 2 + (root // 2**b) % 2) % 2 for b in order]
        below.append([sum(differ[t:]) for t in range(bits)])

    def root_start(q, piece):
        for mirror in range(mirrors):

            @pl.when(below[mirror][0] == 0)
            def _():
                own_copy(mirror, q, piece).start()
                for t in range(bits):
                    branch(mirror, q, piece, t, source(q, piece)).start()

    def relay(mirror, q, piece):
        for t in range(bits):
            copy = branch(mirror, q, piece, t, spot(mirror, q, piece))
            if t == 0:
                copy.wait_recv()

            @pl.when(below[mirror][t] == 0)
            def _():
                copy.start()

    @pl.loop(0, pieces)
    def _(piece):
        value = part[col, piece]
        for step in range(cols - 1):
            to_owner(step * pieces + piece).wait_recv()
            value = value + arrived[step, piece]
        rows_ref[col, piece] = value
        for side in range(2):

            @pl.when((col < cols - 1) if side == 0 else (col > 0))
            def _():
                onward(col, piece, side).start()

    both_sides = jnp.minimum(col, cols - 1 - col)
    longer = jnp.where(2 * col < cols - 1, 1, -1)

    def visit(number):
        group, piece = number // pieces, number % pieces
        paired = group <= 2 * both_sides
        far = jnp.where(paired, (group + 1) // 2, group - both_sides)
        way = jnp.where(paired, 1 - 2 * (group % 2), longer)
        return col + far * way, piece, way

    visits = cols * pieces
    lags = [LAG * below[mirror][0] for mirror in range(mirrors)]

    @pl.loop(0, visits + LAG * bits)
    def _(number):
        q, piece, way = visit(number)

        @pl.when(number < visits)
        def _():
            for side in range(2):

                @pl.when((number >= pieces) & (way == 1 - 2 * (1 - side)))
                def _():
                    copy = onward(q, piece, side)
                    copy.wait_recv()

                    @pl.when((col < cols - 1) if side == 0 else (col > 0))
                    def _():
                        copy.start()

            root_start(q, piece)

        for mirror in range(mirrors):
            late = number - lags[mirror]

            @pl.when((below[mirror][0] != 0) & (late >= 0) & (late < visits))
            def _():
                q, piece, _way = visit(late)
                relay(mirror, q, piece)

    @pl.loop(0, cols)
    def _(q):
        @pl.loop(0, pieces)
        def _(piece):
            @pl.when((q <= col) & (col < cols - 1))
            def _():
                onward(q, piece, 0).wait_send()

            @pl.when((q >= col) & (col > 0))
            def _():
                onward(q, piece, 1).wait_send()

            for mirror in range(mirrors):

                @pl.when(below[mirror][0] == 0)
                def _():
                    own_copy(mirror, q, piece).wait()

                for t in range(bits):

                    @pl.when(below[mirror][t] == 0)
                    def _():
                        branch(mirror, q, piece, t, spot(mirror, q, piece)).wait_send()

    @pl.loop(0, tiles - pieces)
    def _(index):
        to_owner(index).wait_send()

    small = jnp.zeros((width, width), jnp.float32)
    for chunk in range(cyc_cols // tall):
        where = slice(chunk * tall * width, (chunk + 1) * tall * width)
        y = spread_ref[chunk * tall // mirrors : (chunk + 1) * tall // mirrors]
        y = y.reshape(tall * width, width)
        small = small + three_term(split(y), weights[where, :], transposed_left)
    put_half(total_ref, 0, small.T)
    c = first // cols
    y = spread_ref[c // mirrors, c % mirrors]
    put_half(total_ref, 1, jnp.where(col == first % cols, y, 0.0))
    sum_over_col(total_ref, both_ref, *sums)

    if strip is not None:
        strip.end()


def panel_product(matrix, cols, lower, w_top, own, first, old, root_strip, collective_id):
    rows_size, cols_size = lax.axis_size("row"), lax.axis_size("col")
    mirrors = rows_size // cols_size
    bits = rows_size.bit_length() - 1
    cyc_rows, width, cyc_cols, _ = matrix.shape
    n_rows = cyc_rows * width
    depth = n_rows // cols_size
    tile = min(256, depth)
    pieces = depth // tile
    flat = matrix.reshape(n_rows, cyc_cols, width)
    vmem, anywhere = pl.BlockSpec(memory_space=pltpu.VMEM), pl.BlockSpec(memory_space=pl.ANY)
    f32, dma = jnp.float32, pltpu.SemaphoreType.DMA
    args, specs = [flat, cols, lower, w_top, own], [anywhere, vmem, vmem, vmem, vmem]
    if old is not None:
        args += list(old)
        specs += [vmem, vmem]
    out_shape = [
        jax.ShapeDtypeStruct(cols.shape, f32),
        jax.ShapeDtypeStruct((width, width), f32),
        jax.ShapeDtypeStruct((cols_size, pieces, tile, width), f32),
        jax.ShapeDtypeStruct((cyc_rows, mirrors, width, width), f32),
        jax.ShapeDtypeStruct((n_rows, width), f32),
        jax.ShapeDtypeStruct((rows_size, 2 * width // rows_size, width), f32),
    ]
    scratch = [
        pltpu.VMEM((2, cyc_cols, tile, width), f32),
        pltpu.VMEM((cols.shape[0], 2 * width), jnp.bfloat16),
        pltpu.VMEM((cols_size, pieces, tile, width), f32),
        pltpu.VMEM((cols_size - 1, pieces, tile, width), f32),
        dma((2, cyc_cols)),
        dma((cols_size * pieces,)),
        dma((cols_size * pieces,)),
        dma((2, cols_size, pieces)),
        dma((cols_size, pieces)),
        dma((mirrors, cols_size, pieces, bits)),
        dma((mirrors, cols_size, pieces)),
        dma((mirrors, cols_size, pieces)),
    ] + sum_scratch(width)
    if old is not None:
        scratch += [
            pltpu.VMEM((2 * width, width), f32),
            pltpu.VMEM((2 * width, 2 * width), jnp.bfloat16),
        ]
    if root_strip is not None:
        args.append(matrix)
        specs.append(anywhere)
        out_shape.append(jax.ShapeDtypeStruct(matrix.shape[1:], f32))
        scratch += STRIP_SEMS
    return pl.pallas_call(
        functools.partial(
            panel_kernel, first, min(8, cyc_cols), mirrors, old is not None, root_strip
        ),
        out_shape=out_shape,
        in_specs=specs,
        out_specs=[vmem] * len(out_shape),
        scratch_shapes=scratch,
        compiler_params=remote_params(collective_id),
    )(*args)


def update_kernel(
    group,
    a_ref,
    both_ref,
    inverse_ref,
    y_cols_ref,
    w_cols_ref,
    old_cols_ref,
    y_rows_ref,
    w_rows_ref,
    old_rows_ref,
    out_ref,
    held,
    done,
    vh_ref,
    vl_ref,
    finish_ref,
    sems,
    out_sems,
):
    tile = w_rows_ref.shape[0]
    cyc_cols, width = a_ref.shape[1:]
    step, steps = pl.program_id(0), pl.num_programs(0)
    slot, copies = fetch_tiles(a_ref, held, sems, tile)

    @pl.when(step == 0)
    def _():
        inverse = inverse_ref[...]
        core = 0.5 * transposed_dot(dot_highest(inverse, get_half(both_ref, 0)), inverse)
        finish_ref[...] = side_by_side(jnp.concatenate([inverse.T, -core], axis=0))
        rows = min(4, cyc_cols) * width

        @pl.loop(0, cyc_cols * width // rows)
        def _(chunk):
            where = pl.ds(pl.multiple_of(chunk * rows, rows), rows)
            w = w_cols_ref[where, :]
            z = three_term(
                split(jnp.concatenate([y_cols_ref[where, :], w], axis=1)), finish_ref[...], dot_f32
            )
            for at, value in ((0, old_cols_ref[where, :]), (2 * width, w), (3 * width, z)):
                v_high, v_low = split(value.T)
                vh_ref[at : at + value.shape[1], where] = v_high
                vl_ref[at : at + value.shape[1], where] = v_low

    w = w_rows_ref[...]
    z = three_term(
        split(jnp.concatenate([y_rows_ref[...], w], axis=1)), finish_ref[...], dot_f32
    )
    high, low = split(jnp.concatenate([old_rows_ref[...], z, w], axis=1))

    def stores(index, where):
        return [
            pltpu.make_async_copy(
                done.at[where, c],
                out_ref.at[pl.ds(index * tile, tile), c, :],
                out_sems.at[where, c],
            )
            for c in range(cyc_cols)
        ]

    @pl.when(step >= 2)
    def _():
        for copy in stores(step - 2, slot):
            copy.wait()

    for copy in copies:
        copy.wait()
    started = stores(step, slot)
    for chunk in range(cyc_cols // group):
        columns = slice(chunk * group * width, (chunk + 1) * group * width)
        v_high, v_low = vh_ref[:, columns], vl_ref[:, columns]
        delta = dot_f32(high, v_low) + dot_f32(low, v_high) + dot_f32(high, v_high)
        for g in range(group):
            c = chunk * group + g
            done[slot, c] = held[slot, c] - delta[:, g * width : (g + 1) * width]
            started[c].start()

    @pl.when(step == steps - 1)
    def _():
        for copy in stores(step, slot):
            copy.wait()

        @pl.when(steps > 1)
        def _():
            for copy in stores(step - 1, 1 - slot):
                copy.wait()


def apply_update(matrix, both, inverse, y_cols, w_cols, old_cols, y_rows, w_rows, old_rows):
    cyc_rows, width, cyc_cols, _ = matrix.shape
    n_rows = cyc_rows * width
    tile = min(256, n_rows)

    def whole(x):
        return pl.BlockSpec(x.shape, lambda i: (0,) * x.ndim, pipeline_mode=pl.Buffered(1))

    def some(x):
        return pl.BlockSpec((tile, x.shape[1]), lambda i: (i, 0))

    held = pltpu.VMEM((2, cyc_cols, tile, width), jnp.float32)
    right = pltpu.VMEM((4 * width, cyc_cols * width), jnp.bfloat16)
    sems = pltpu.SemaphoreType.DMA((2, cyc_cols))
    fixed, moving = [both, inverse, y_cols, w_cols, old_cols], [y_rows, w_rows, old_rows]
    return pl.pallas_call(
        functools.partial(update_kernel, min(4, cyc_cols)),
        grid=(n_rows // tile,),
        out_shape=jax.ShapeDtypeStruct((n_rows, cyc_cols, width), jnp.float32),
        in_specs=[pl.BlockSpec(memory_space=pl.ANY)]
        + [whole(x) for x in fixed]
        + [some(x) for x in moving],
        out_specs=pl.BlockSpec(memory_space=pl.ANY),
        scratch_shapes=[
            held,
            held,
            right,
            right,
            pltpu.VMEM((2 * width, 2 * width), jnp.bfloat16),
            sems,
            sems,
        ],
        compiler_params=pltpu.CompilerParams(vmem_limit_bytes=VMEM_LIMIT),
    )(matrix.reshape(n_rows, cyc_cols, width), *fixed, *moving)


def local(matrix):
    row_count = lax.axis_size("row")
    col_count = lax.axis_size("col")
    cyc_rows, width, cyc_cols, _ = matrix.shape
    n_rows, n_cols = cyc_rows * width, cyc_cols * width

    strip, raw = spread(matrix, 0, 0, 0, 0, 0)
    cols, own, lower, w_top, raw = prepare(
        strip, raw, 1, None, matrix, (1 % col_count, 1 // col_count), 1
    )
    strip_of = (1 % row_count, 1 // row_count)
    wc, inverse, y_rows, y_cols, wr, both, strip = panel_product(
        matrix, cols, lower, w_top, own, 1, None, strip_of, 2
    )
    later = [
        both,
        inverse,
        w_top,
        y_cols.reshape(n_cols, width),
        wc,
        y_rows.reshape(n_rows, width),
        wr,
    ]
    cols, own, lower, w_top, old_cols, old_rows = prepare(strip, raw, 2, later, matrix, None, 3)
    wc, inverse, y_rows, y_cols, wr_last, both = panel_product(
        matrix, cols, lower, w_top, own, 2, (old_cols, old_rows), None, 4
    )
    y_rows, y_cols = y_rows.reshape(n_rows, width), y_cols.reshape(n_cols, width)
    reduced = apply_update(
        matrix, both, inverse, y_cols, wc, old_cols, y_rows, wr_last, old_rows
    ).reshape(matrix.shape)
    bases = jnp.concatenate([wr, wr_last], axis=1).reshape(cyc_rows, width, PANELS * width)
    return (reduced, bases)


def solution(mesh):
    return jax.shard_map(
        local,
        mesh=mesh,
        in_specs=(P(None, "row", None, "col"),),
        out_specs=(P(None, "row", None, "col"), P(None, "row", None)),
        check_vma=False,
    )
```
